128 devices in a mesh: dp: 16 (over x, z), tensor: 8 (over y, core).
Axes of the slice: x: 4, y: 4, z: 4, core: 2. Of those that a mesh axis runs over, the one named last changes fastest.
Arguments:
- attn_norm_grad: bfloat16 [16, 2048], P('dp', 'tensor'), may hold values from -1.5 to 1.5
- query_grad: bfloat16 [16, 2048, 2048], P('dp', None, 'tensor'), may hold values from -1.5 to 1.5
- forget_grad: bfloat16 [16, 2048, 2048], P('dp', None, 'tensor'), may hold values from -1.5 to 1.5
- input_grad: bfloat16 [16, 2048, 2048], P('dp', None, 'tensor'), may hold values from -1.5 to 1.5
- group_norm_grad: bfloat16 [16, 2048], P('dp', 'tensor'), may hold values from -1.5 to 1.5
- output_gate_grad: bfloat16 [16, 2048, 2048], P('dp', None, 'tensor'), may hold values from -1.5 to 1.5
- out_proj_grad: bfloat16 [16, 2048, 2048], P('dp', 'tensor'), may hold values from -1.5 to 1.5
- mlp_norm_grad: bfloat16 [16, 2048], P('dp', 'tensor'), may hold values from -1.5 to 1.5
- gate_proj_grad: bfloat16 [16, 2048, 2816], P('dp', None, 'tensor'), may hold values from -1.5 to 1.5
- up_proj_grad: bfloat16 [16, 2048, 2816], P('dp', None, 'tensor'), may hold values from -1.5 to 1.5
- down_proj_grad: bfloat16 [16, 2816, 2048], P('dp', 'tensor'), may hold values from -1.5 to 1.5
- weights: float32 [8, 4784896], P('tensor', 'dp'), as said below
- first_moment: float32 [8, 4784896], P('tensor', 'dp'), may hold values from -0.6 to 0.6
- second_moment: float32 [8, 4784896], P('tensor', 'dp'), may hold values from 0.001 to 1
Outputs:
- new_weights: float32 [8, 4784896], P('tensor', 'dp')
- new_first: float32 [8, 4784896], P('tensor', 'dp')
- new_second: float32 [8, 4784896], P('tensor', 'dp')
- attn_norm_copy: bfloat16 [2048], P('tensor')
- query_copy: bfloat16 [2048, 2048], P(None, 'tensor')
- forget_copy: bfloat16 [2048, 2048], P(None, 'tensor')
- input_copy: bfloat16 [2048, 2048], P(None, 'tensor')
- group_norm_copy: bfloat16 [2048], P('tensor')
- output_gate_copy: bfloat16 [2048, 2048], P(None, 'tensor')
- out_proj_copy: bfloat16 [2048, 2048], P('tensor')
- mlp_norm_copy: bfloat16 [2048], P('tensor')
- gate_proj_copy: bfloat16 [2048, 2816], P(None, 'tensor')
- up_proj_copy: bfloat16 [2048, 2816], P(None, 'tensor')
- down_proj_copy: bfloat16 [2816, 2048], P('tensor')
The draws below stay inside these ranges and needn't reach their ends.
Inputs may be any that keep to these rules, and one draw needn't show every extreme that they name: float32 master weights of order one.
All inputs are finite; a program needn't handle non-finite values.
Results may differ from the reference program's by a relative error of at most 0.0085.
Values may be sent and summed in bfloat16 or wider, within the bound.
A program may use at most 192 MiB of HBM per device.

```python
import math
import jax
import jax.numpy as jnp
import numpy as np
from jax import lax

D = 2048
FF = 2816
SHARDS = 16
GROUPS = 8
LOCAL = 4784896


def draw_weights(key, part):
    rise = 1.0 + 2.0 * jnp.arange(LOCAL, dtype=jnp.float32) / LOCAL
    return jax.random.normal(key, (GROUPS, LOCAL), jnp.float32) * rise[None, :]


def steps_of(stream_key, dims, shards, smallest, high):
    loudness = 1.0
    for dim, blocks in shards:
        steps = jax.random.uniform(jax.random.fold_in(jax.random.fold_in(stream_key, 6), dim), (blocks,), jnp.float32, smallest / len(shards), high / len(shards))
        loudness = loudness * jnp.repeat(jnp.exp(steps), dims[dim] // blocks).reshape((-1,) + (1,) * (len(dims) - 1 - dim))
    return loudness


def scatter_about(stream_key, extent, deviation, reach, split=(), kind=jnp.bfloat16):
    level = steps_of(stream_key, extent, split, -0.22, 0.18) if split else 1.0
    result = jax.random.normal(stream_key, extent, jnp.float32) * deviation * level
    return jnp.minimum(jnp.maximum(result, -reach), reach).astype(kind)


def setup_inputs(seed: int = 0) -> dict:
    splits = jax.random.split(jax.random.key(seed), 15)
    return {
        "attn_norm_grad": scatter_about(splits[0], (SHARDS, D), 0.25, 1.5, ((0, 16), (1, 8))),
        "query_grad": scatter_about(splits[1], (SHARDS, D, D), 0.25, 1.5, ((0, 16), (2, 8))),
        "forget_grad": scatter_about(splits[2], (SHARDS, D, D), 0.25, 1.5, ((0, 16), (2, 8))),
        "input_grad": scatter_about(splits[3], (SHARDS, D, D), 0.25, 1.5, ((0, 16), (2, 8))),
        "group_norm_grad": scatter_about(splits[4], (SHARDS, D), 0.25, 1.5, ((0, 16), (1, 8))),
        "output_gate_grad": scatter_about(splits[5], (SHARDS, D, D), 0.25, 1.5, ((0, 16), (2, 8))),
        "out_proj_grad": scatter_about(splits[6], (SHARDS, D, D), 0.25, 1.5, ((0, 16), (1, 8))),
        "mlp_norm_grad": scatter_about(splits[7], (SHARDS, D), 0.25, 1.5, ((0, 16), (1, 8))),
        "gate_proj_grad": scatter_about(splits[8], (SHARDS, D, FF), 0.25, 1.5, ((0, 16), (2, 8))),
        "up_proj_grad": scatter_about(splits[9], (SHARDS, D, FF), 0.25, 1.5, ((0, 16), (2, 8))),
        "down_proj_grad": scatter_about(splits[10], (SHARDS, FF, D), 0.25, 1.5, ((0, 16), (1, 8))),
        "weights": draw_weights(jax.random.fold_in(splits[14], 71), 0),
        "first_moment": scatter_about(splits[12], (GROUPS, LOCAL), 0.1, 0.6, ((0, 8), (1, 16)), jnp.float32),
        "second_moment": jnp.clip(jnp.exp(math.log(1.0) - 6.9077552 * jax.random.uniform(splits[13], (GROUPS, LOCAL), jnp.float32) ** steps_of(splits[13], (GROUPS, LOCAL), ((0, 8), (1, 16)), -0.2, 0.2)), 0.001, 1.0),
    }


KINDS = ('gain', 'last', 'last', 'last', 'gain', 'last', 'first', 'gain', 'last', 'last', 'first')
GAIN_SEGMENTS = (0, 4, 7)

def block_of(array, kind, index, groups):
    if kind == 'last':
        width = array.shape[1] // groups
        return array[:, index * width:(index + 1) * width]
    width = array.shape[0] // groups
    return array[index * width:(index + 1) * width]

def flat_row(arrays, index):
    pieces = [block_of(arrays[k], KINDS[k], index, GROUPS).reshape(SHARDS, -1) for k in range(11)]
    return jnp.concatenate([pieces[k][j] for j in range(SHARDS) for k in range(11)])

def rebuild(flat_rows, params, lengths):
    piece_len = [n // SHARDS for n in lengths]
    stride = sum(piece_len)
    starts = [sum(piece_len[:k]) for k in range(11)]
    outputs = []
    for number in range(11):
        kind = KINDS[number]
        blocks = []
        for index in range(GROUPS):
            shape = block_of(params[number], kind, index, GROUPS).shape
            parts = [flat_rows[index, j * stride + starts[number]:j * stride + starts[number] + piece_len[number]] for j in range(SHARDS)]
            blocks.append(jnp.concatenate(parts).reshape(shape))
        axis = 1 if kind == 'last' else 0
        outputs.append(jnp.concatenate(blocks, axis=axis))
    return outputs

def reference(attn_norm_grad, query_grad, forget_grad, input_grad, group_norm_grad, output_gate_grad, out_proj_grad, mlp_norm_grad, gate_proj_grad, up_proj_grad, down_proj_grad, weights, first_moment, second_moment):
    grads = (attn_norm_grad, query_grad, forget_grad, input_grad, group_norm_grad, output_gate_grad, out_proj_grad, mlp_norm_grad, gate_proj_grad, up_proj_grad, down_proj_grad)
    summed = [lax.optimization_barrier(jnp.sum(g.astype(jnp.float32), axis=0)) for g in grads]
    lengths = [block_of(summed[k], KINDS[k], 0, GROUPS).size for k in range(11)]
    grad = jnp.stack([flat_row(summed, index) for index in range(GROUPS)])
    piece_len = [n // SHARDS for n in lengths]
    segment = np.tile(np.repeat(np.arange(11), piece_len), SHARDS).astype(np.int32)
    is_gain = np.isin(segment, np.array(GAIN_SEGMENTS)).astype(np.float32)
    matrix_mask = jnp.asarray(1.0 - is_gain, dtype=jnp.float32)[None, :]
    new_first = 0.9 * first_moment + 0.1 * grad
    new_second = 0.999 * second_moment + 0.001 * grad * grad
    update = new_first / (jnp.sqrt(new_second) + 1e-06) + 0.01 * weights * matrix_mask
    ids = jnp.asarray(np.tile(segment, GROUPS), dtype=jnp.int32)
    weight_sq = jax.ops.segment_sum((weights * weights).reshape(-1), ids, 11)
    update_sq = jax.ops.segment_sum((update * update).reshape(-1), ids, 11)
    trust = jnp.sqrt(weight_sq) / jnp.sqrt(update_sq)
    scale = trust[jnp.asarray(segment, dtype=jnp.int32)][None, :]
    new_weights = weights - 0.1 * scale * update
    copies = rebuild(new_weights.astype(jnp.bfloat16), summed, lengths)
    return (new_weights, new_first, new_second, copies[0], copies[1], copies[2], copies[3], copies[4], copies[5], copies[6], copies[7], copies[8], copies[9], copies[10])
```

```python
import jax
import jax.numpy as jnp
from jax import lax
from jax.sharding import PartitionSpec as P

GAIN_SEGMENTS = (0, 4, 7)


def on_device(*args):
    grads = args[:11]
    weights, first_moment, second_moment = args[11:]
    owners = lax.axis_size("dp")
    shapes = [g.shape[1:] for g in grads]
    pieces = [g.reshape(owners, -1) for g in grads]
    piece_len = [p.shape[1] for p in pieces]
    starts = [sum(piece_len[:k]) for k in range(11)]
    own_count = sum(piece_len)
    padded = -(-own_count // 1024) * 1024
    pad = jnp.zeros((owners, padded - own_count), grads[0].dtype)
    flat = jnp.concatenate(pieces + [pad], axis=1).reshape(owners, padded // 128, 128)
    grad = lax.psum_scatter(flat, "dp", scatter_dimension=0, tiled=True)
    grad = grad.reshape(-1)[:own_count].astype(jnp.float32)
    weight_row = weights.reshape(-1)
    first_row = first_moment.reshape(-1)
    second_row = second_moment.reshape(-1)
    new_first = 0.9 * first_row + 0.1 * grad
    new_second = 0.999 * second_row + 0.001 * grad * grad
    updates = []
    weight_parts = []
    for k in range(11):
        w = weight_row[starts[k] : starts[k] + piece_len[k]]
        f = new_first[starts[k] : starts[k] + piece_len[k]]
        s = new_second[starts[k] : starts[k] + piece_len[k]]
        u = f / (jnp.sqrt(s) + 1e-06)
        if k not in GAIN_SEGMENTS:
            u = u + 0.01 * w
        updates.append(u)
        weight_parts.append(w)
    sums = jnp.stack(
        [jnp.sum(w * w) for w in weight_parts] + [jnp.sum(u * u) for u in updates]
    )
    sums = lax.psum(sums, ("dp", "tensor"))
    trust = jnp.sqrt(sums[:11]) / jnp.sqrt(sums[11:])
    new_parts = [
        weight_parts[k] - 0.1 * trust[k] * updates[k] for k in range(11)
    ]
    new_weights = jnp.concatenate(new_parts)
    rounded = new_weights.astype(jnp.bfloat16)
    gathered = lax.all_gather(rounded, "dp", axis=0, tiled=False)
    copies = [
        gathered[:, starts[k] : starts[k] + piece_len[k]].reshape(shapes[k])
        for k in range(11)
    ]
    return (
        new_weights.reshape(1, -1),
        new_first.reshape(1, -1),
        new_second.reshape(1, -1),
        *copies,
    )


def solution(mesh):
    return jax.shard_map(
        on_device,
        mesh=mesh,
        in_specs=(
            P("dp", "tensor"),
            P("dp", None, "tensor"),
            P("dp", None, "tensor"),
            P("dp", None, "tensor"),
            P("dp", "tensor"),
            P("dp", None, "tensor"),
            P("dp", "tensor", None),
            P("dp", "tensor"),
            P("dp", None, "tensor"),
            P("dp", None, "tensor"),
            P("dp", "tensor", None),
            P("tensor", "dp"),
            P("tensor", "dp"),
            P("tensor", "dp"),
        ),
        out_specs=(
            P("tensor", "dp"),
            P("tensor", "dp"),
            P("tensor", "dp"),
            P("tensor"),
            P(None, "tensor"),
            P(None, "tensor"),
            P(None, "tensor"),
            P("tensor"),
            P(None, "tensor"),
            P("tensor", None),
            P("tensor"),
            P(None, "tensor"),
            P(None, "tensor"),
            P("tensor", None),
        ),
        check_vma=False,
    )
```

```python
import jax
import jax.numpy as jnp
from jax import lax
from jax.sharding import PartitionSpec as P

GAIN_SEGMENTS = (0, 4, 7)


def on_device(*args):
    grads = args[:11]
    weights, first_moment, second_moment = args[11:]
    owners = lax.axis_size("dp")
    shapes = [g.shape[1:] for g in grads]
    pieces = [g.reshape(owners, -1) for g in grads]
    piece_len = [p.shape[1] for p in pieces]
    starts = [sum(piece_len[:k]) for k in range(11)]
    own_count = sum(piece_len)
    order = [k for k in range(11) if k not in GAIN_SEGMENTS] + list(GAIN_SEGMENTS)
    packed_len = sum(piece_len)
    padded = -(-packed_len // 1024) * 1024
    pad = jnp.zeros((owners, padded - packed_len), grads[0].dtype)
    flat = jnp.concatenate([pieces[k] for k in order] + [pad], axis=1)
    flat = flat.reshape(owners, padded // 128, 128)
    summed = lax.psum_scatter(flat, "dp", scatter_dimension=0, tiled=True)
    summed = lax.optimization_barrier(summed).reshape(-1)
    packed_start = {}
    offset = 0
    for k in order:
        packed_start[k] = offset
        offset += piece_len[k]
    grad = jnp.concatenate(
        [summed[packed_start[k] : packed_start[k] + piece_len[k]] for k in range(11)]
    ).astype(jnp.float32)
    weight_row = weights.reshape(-1)
    first_row = first_moment.reshape(-1)
    second_row = second_moment.reshape(-1)
    new_first = 0.9 * first_row + 0.1 * grad
    new_second = 0.999 * second_row + 0.001 * grad * grad
    updates = []
    weight_parts = []
    for k in range(11):
        w = weight_row[starts[k] : starts[k] + piece_len[k]]
        f = new_first[starts[k] : starts[k] + piece_len[k]]
        s = new_second[starts[k] : starts[k] + piece_len[k]]
        u = f / (jnp.sqrt(s) + 1e-06)
        if k not in GAIN_SEGMENTS:
            u = u + 0.01 * w
        updates.append(u)
        weight_parts.append(w)
    sums = lax.psum(
        [jnp.sum(w * w) for w in weight_parts] + [jnp.sum(u * u) for u in updates],
        ("dp", "tensor"),
    )
    trust = [jnp.sqrt(sums[k]) / jnp.sqrt(sums[11 + k]) for k in range(11)]
    new_parts = [
        weight_parts[k] - 0.1 * trust[k] * updates[k] for k in range(11)
    ]
    new_weights = jnp.concatenate(new_parts)
    rounded = jnp.concatenate(
        [new_parts[k].astype(jnp.bfloat16) for k in order]
        + [jnp.zeros((padded - packed_len,), jnp.bfloat16)]
    )
    gathered = lax.all_gather(rounded.reshape(padded // 128, 128), "dp", axis=0, tiled=False)
    gathered = gathered.reshape(owners, padded)
    copies = [None] * 11
    for k in range(11):
        part = gathered[:, packed_start[k] : packed_start[k] + piece_len[k]]
        copies[k] = part.reshape(shapes[k])
    return (
        new_weights.reshape(1, -1),
        new_first.reshape(1, -1),
        new_second.reshape(1, -1),
        *copies,
    )


def solution(mesh):
    return jax.shard_map(
        on_device,
        mesh=mesh,
        in_specs=(
            P("dp", "tensor"),
            P("dp", None, "tensor"),
            P("dp", None, "tensor"),
            P("dp", None, "tensor"),
            P("dp", "tensor"),
            P("dp", None, "tensor"),
            P("dp", "tensor", None),
            P("dp", "tensor"),
            P("dp", None, "tensor"),
            P("dp", None, "tensor"),
            P("dp", "tensor", None),
            P("tensor", "dp"),
            P("tensor", "dp"),
            P("tensor", "dp"),
        ),
        out_specs=(
            P("tensor", "dp"),
            P("tensor", "dp"),
            P("tensor", "dp"),
            P("tensor"),
            P(None, "tensor"),
            P(None, "tensor"),
            P(None, "tensor"),
            P("tensor"),
            P(None, "tensor"),
            P("tensor", None),
            P("tensor"),
            P(None, "tensor"),
            P(None, "tensor"),
            P("tensor", None),
        ),
        check_vma=False,
    )
```

```python
import functools

import jax
import jax.numpy as jnp
from jax import lax
from jax.experimental import pallas as pl
from jax.experimental.pallas import tpu as pltpu
from jax.sharding import PartitionSpec as P

MESH = pl.DeviceIdType.MESH

GAIN_SEGMENTS = (0, 4, 7)


def norm_kernel(nd, nt, count, *refs):
    scalars = refs[:count]
    out_ref = refs[count]
    recv_a, recv_b, send_a, got_a, send_b, got_b = refs[count + 1 :]
    d = lax.axis_index("dp")
    t = lax.axis_index("tensor")
    barrier = pltpu.get_barrier_semaphore()
    for step in range(1, nt):
        pl.semaphore_signal(
            barrier, inc=1, device_id=(d, lax.rem(t + step, nt)), device_id_type=MESH
        )
    for step in range(1, nd):
        pl.semaphore_signal(
            barrier, inc=1, device_id=(lax.rem(d + step, nd), t), device_id_type=MESH
        )
    pl.semaphore_wait(barrier, nt - 1 + nd - 1)
    row = lax.broadcasted_iota(jnp.int32, (8, 128), 0)
    lane = lax.broadcasted_iota(jnp.int32, (8, 128), 1)
    half = count // 2
    vec = jnp.zeros((8, 128), jnp.float32)
    for k in range(count):
        hit = (row == k // half) & (lane == k % half)
        vec = jnp.where(hit, scalars[k][0, 0], vec)
    recv_a[t] = vec
    copies = []
    for step in range(1, nt):
        copy = pltpu.make_async_remote_copy(
            src_ref=recv_a.at[t],
            dst_ref=recv_a.at[t],
            send_sem=send_a.at[step],
            recv_sem=got_a.at[t],
            device_id=(d, lax.rem(t + step, nt)),
            device_id_type=MESH,
        )
        copy.start()
        copies.append(copy)
    for step in range(1, nt):
        source = lax.rem(t + nt - step, nt)
        pltpu.make_async_remote_copy(
            src_ref=recv_a.at[source],
            dst_ref=recv_a.at[source],
            send_sem=send_a.at[step],
            recv_sem=got_a.at[source],
            device_id=(d, source),
            device_id_type=MESH,
        ).wait_recv()
    for copy in copies:
        copy.wait_send()
    acc = recv_a[0]
    for slot in range(1, nt):
        acc = acc + recv_a[slot]
    recv_b[d] = acc
    copies = []
    for step in range(1, nd):
        copy = pltpu.make_async_remote_copy(
            src_ref=recv_b.at[d],
            dst_ref=recv_b.at[d],
            send_sem=send_b.at[step],
            recv_sem=got_b.at[d],
            device_id=(lax.rem(d + step, nd), t),
            device_id_type=MESH,
        )
        copy.start()
        copies.append(copy)
    for step in range(1, nd):
        source = lax.rem(d + nd - step, nd)
        pltpu.make_async_remote_copy(
            src_ref=recv_b.at[source],
            dst_ref=recv_b.at[source],
            send_sem=send_b.at[step],
            recv_sem=got_b.at[source],
            device_id=(source, t),
            device_id_type=MESH,
        ).wait_recv()
    for copy in copies:
        copy.wait_send()
    acc = recv_b[0]
    for slot in range(1, nd):
        acc = acc + recv_b[slot]
    out_ref[...] = acc


def global_sums(values):
    nd = lax.axis_size("dp")
    nt = lax.axis_size("tensor")
    count = len(values)
    return pl.pallas_call(
        functools.partial(norm_kernel, nd, nt, count),
        out_shape=jax.ShapeDtypeStruct((8, 128), jnp.float32),
        in_specs=[pl.BlockSpec(memory_space=pltpu.SMEM)] * count,
        out_specs=pl.BlockSpec(memory_space=pltpu.VMEM),
        scratch_shapes=[
            pltpu.VMEM((nt, 8, 128), jnp.float32),
            pltpu.VMEM((nd, 8, 128), jnp.float32),
            pltpu.SemaphoreType.DMA((nt,)),
            pltpu.SemaphoreType.DMA((nt,)),
            pltpu.SemaphoreType.DMA((nd,)),
            pltpu.SemaphoreType.DMA((nd,)),
        ],
        compiler_params=pltpu.CompilerParams(collective_id=0, has_side_effects=True),
    )(*[v.reshape(1, 1) for v in values])


def on_device(*args):
    grads = args[:11]
    weights, first_moment, second_moment = args[11:]
    owners = lax.axis_size("dp")
    shapes = [g.shape[1:] for g in grads]
    pieces = [g.reshape(owners, -1) for g in grads]
    piece_len = [p.shape[1] for p in pieces]
    starts = [sum(piece_len[:k]) for k in range(11)]
    own_count = sum(piece_len)
    order = [k for k in range(11) if k not in GAIN_SEGMENTS] + list(GAIN_SEGMENTS)
    packed_len = sum(piece_len)
    padded = -(-packed_len // 1024) * 1024
    pad = jnp.zeros((owners, padded - packed_len), grads[0].dtype)
    flat = jnp.concatenate([pieces[k] for k in order] + [pad], axis=1)
    flat = flat.reshape(owners, padded // 128, 128)
    summed = lax.psum_scatter(flat, "dp", scatter_dimension=0, tiled=True)
    summed = lax.optimization_barrier(summed).reshape(-1)
    packed_start = {}
    offset = 0
    for k in order:
        packed_start[k] = offset
        offset += piece_len[k]
    grad = jnp.concatenate(
        [summed[packed_start[k] : packed_start[k] + piece_len[k]] for k in range(11)]
    ).astype(jnp.float32)
    weight_row = weights.reshape(-1)
    first_row = first_moment.reshape(-1)
    second_row = second_moment.reshape(-1)
    new_first = 0.9 * first_row + 0.1 * grad
    new_second = 0.999 * second_row + 0.001 * grad * grad
    updates = []
    weight_parts = []
    for k in range(11):
        w = weight_row[starts[k] : starts[k] + piece_len[k]]
        f = new_first[starts[k] : starts[k] + piece_len[k]]
        s = new_second[starts[k] : starts[k] + piece_len[k]]
        u = f / (jnp.sqrt(s) + 1e-06)
        if k not in GAIN_SEGMENTS:
            u = u + 0.01 * w
        updates.append(u)
        weight_parts.append(w)
    sums = global_sums(
        [jnp.sum(w * w) for w in weight_parts] + [jnp.sum(u * u) for u in updates]
    )
    trust = [jnp.sqrt(sums[0, k]) / jnp.sqrt(sums[1, k]) for k in range(11)]
    new_parts = [
        weight_parts[k] - 0.1 * trust[k] * updates[k] for k in range(11)
    ]
    new_weights = jnp.concatenate(new_parts)
    rounded = jnp.concatenate(
        [new_parts[k].astype(jnp.bfloat16) for k in order]
        + [jnp.zeros((padded - packed_len,), jnp.bfloat16)]
    )
    gathered = lax.all_gather(rounded.reshape(padded // 128, 128), "dp", axis=0, tiled=False)
    gathered = gathered.reshape(owners, padded)
    copies = [None] * 11
    for k in range(11):
        part = gathered[:, packed_start[k] : packed_start[k] + piece_len[k]]
        copies[k] = part.reshape(shapes[k])
    return (
        new_weights.reshape(1, -1),
        new_first.reshape(1, -1),
        new_second.reshape(1, -1),
        *copies,
    )


def solution(mesh):
    return jax.shard_map(
        on_device,
        mesh=mesh,
        in_specs=(
            P("dp", "tensor"),
            P("dp", None, "tensor"),
            P("dp", None, "tensor"),
            P("dp", None, "tensor"),
            P("dp", "tensor"),
            P("dp", None, "tensor"),
            P("dp", "tensor", None),
            P("dp", "tensor"),
            P("dp", None, "tensor"),
            P("dp", None, "tensor"),
            P("dp", "tensor", None),
            P("tensor", "dp"),
            P("tensor", "dp"),
            P("tensor", "dp"),
        ),
        out_specs=(
            P("tensor", "dp"),
            P("tensor", "dp"),
            P("tensor", "dp"),
            P("tensor"),
            P(None, "tensor"),
            P(None, "tensor"),
            P(None, "tensor"),
            P("tensor"),
            P(None, "tensor"),
            P("tensor", None),
            P("tensor"),
            P(None, "tensor"),
            P(None, "tensor"),
            P("tensor", None),
        ),
        check_vma=False,
    )
```

```python
import functools

import jax
import jax.numpy as jnp
from jax import lax
from jax.experimental import pallas as pl
from jax.experimental.pallas import tpu as pltpu
from jax.sharding import PartitionSpec as P

MESH = pl.DeviceIdType.MESH

GAIN_SEGMENTS = (0, 4, 7)


def norm_kernel(nd, nt, count, *refs):
    scalars = refs[:count]
    out_ref = refs[count]
    recv_a, recv_b, send_a, got_a, send_b, got_b = refs[count + 1 :]
    d = lax.axis_index("dp")
    t = lax.axis_index("tensor")
    barrier = pltpu.get_barrier_semaphore()
    for step in range(1, nt):
        pl.semaphore_signal(
            barrier, inc=1, device_id=(d, lax.rem(t + step, nt)), device_id_type=MESH
        )
    for step in range(1, nd):
        pl.semaphore_signal(
            barrier, inc=1, device_id=(lax.rem(d + step, nd), t), device_id_type=MESH
        )
    pl.semaphore_wait(barrier, nt - 1 + nd - 1)
    row = lax.broadcasted_iota(jnp.int32, (8, 128), 0)
    lane = lax.broadcasted_iota(jnp.int32, (8, 128), 1)
    half = count // 2
    vec = jnp.zeros((8, 128), jnp.float32)
    for k in range(count):
        hit = (row == k // half) & (lane == k % half)
        vec = jnp.where(hit, scalars[k][0, 0], vec)
    recv_a[t] = vec
    copies = []
    for step in range(1, nt):
        copy = pltpu.make_async_remote_copy(
            src_ref=recv_a.at[t],
            dst_ref=recv_a.at[t],
            send_sem=send_a.at[step],
            recv_sem=got_a.at[t],
            device_id=(d, lax.rem(t + step, nt)),
            device_id_type=MESH,
        )
        copy.start()
        copies.append(copy)
    for step in range(1, nt):
        source = lax.rem(t + nt - step, nt)
        pltpu.make_async_remote_copy(
            src_ref=recv_a.at[source],
            dst_ref=recv_a.at[source],
            send_sem=send_a.at[step],
            recv_sem=got_a.at[source],
            device_id=(d, source),
            device_id_type=MESH,
        ).wait_recv()
    for copy in copies:
        copy.wait_send()
    acc = recv_a[0]
    for slot in range(1, nt):
        acc = acc + recv_a[slot]
    recv_b[d] = acc
    copies = []
    for step in range(1, nd):
        copy = pltpu.make_async_remote_copy(
            src_ref=recv_b.at[d],
            dst_ref=recv_b.at[d],
            send_sem=send_b.at[step],
            recv_sem=got_b.at[d],
            device_id=(lax.rem(d + step, nd), t),
            device_id_type=MESH,
        )
        copy.start()
        copies.append(copy)
    for step in range(1, nd):
        source = lax.rem(d + nd - step, nd)
        pltpu.make_async_remote_copy(
            src_ref=recv_b.at[source],
            dst_ref=recv_b.at[source],
            send_sem=send_b.at[step],
            recv_sem=got_b.at[source],
            device_id=(source, t),
            device_id_type=MESH,
        ).wait_recv()
    for copy in copies:
        copy.wait_send()
    acc = recv_b[0]
    for slot in range(1, nd):
        acc = acc + recv_b[slot]
    out_ref[...] = acc


def global_sums(values):
    nd = lax.axis_size("dp")
    nt = lax.axis_size("tensor")
    count = len(values)
    return pl.pallas_call(
        functools.partial(norm_kernel, nd, nt, count),
        out_shape=jax.ShapeDtypeStruct((8, 128), jnp.float32),
        in_specs=[pl.BlockSpec(memory_space=pltpu.SMEM)] * count,
        out_specs=pl.BlockSpec(memory_space=pltpu.VMEM),
        scratch_shapes=[
            pltpu.VMEM((nt, 8, 128), jnp.float32),
            pltpu.VMEM((nd, 8, 128), jnp.float32),
            pltpu.SemaphoreType.DMA((nt,)),
            pltpu.SemaphoreType.DMA((nt,)),
            pltpu.SemaphoreType.DMA((nd,)),
            pltpu.SemaphoreType.DMA((nd,)),
        ],
        compiler_params=pltpu.CompilerParams(collective_id=0, has_side_effects=True),
    )(*[v.reshape(1, 1) for v in values])


def on_device(*args):
    grads = args[:11]
    weights, first_moment, second_moment = args[11:]
    owners = lax.axis_size("dp")
    shapes = [g.shape[1:] for g in grads]
    pieces = [g.reshape(owners, -1) for g in grads]
    piece_len = [p.shape[1] for p in pieces]
    starts = [sum(piece_len[:k]) for k in range(11)]
    own_count = sum(piece_len)
    order = [k for k in range(11) if k not in GAIN_SEGMENTS] + list(GAIN_SEGMENTS)
    packed_len = sum(piece_len)
    padded = -(-packed_len // 1024) * 1024
    pad = jnp.zeros((owners, padded - packed_len), grads[0].dtype)
    flat = jnp.concatenate([pieces[k] for k in order] + [pad], axis=1)
    flat = flat.reshape(owners, padded // 128, 128)
    summed = lax.psum_scatter(flat, "dp", scatter_dimension=0, tiled=True)
    summed = lax.optimization_barrier(summed).reshape(-1)
    packed_start = {}
    offset = 0
    for k in order:
        packed_start[k] = offset
        offset += piece_len[k]
    rows = padded // 128

    def to_packed(row):
        parts = [row[starts[k] : starts[k] + piece_len[k]] for k in order]
        parts.append(jnp.zeros((padded - packed_len,), row.dtype))
        return jnp.concatenate(parts).reshape(rows, 128)

    def to_flat(block):
        row = block.reshape(-1)
        parts = [row[packed_start[k] : packed_start[k] + piece_len[k]] for k in range(11)]
        return jnp.concatenate(parts).reshape(1, -1)

    grad = summed.reshape(rows, 128).astype(jnp.float32)
    weight_p = to_packed(weights.reshape(-1))
    first_p = to_packed(first_moment.reshape(-1))
    second_p = to_packed(second_moment.reshape(-1))
    new_first = 0.9 * first_p + 0.1 * grad
    new_second = 0.999 * second_p + 0.001 * grad * grad
    position = (
        lax.broadcasted_iota(jnp.int32, (rows, 128), 0) * 128
        + lax.broadcasted_iota(jnp.int32, (rows, 128), 1)
    )
    big_end = min(packed_start[k] for k in GAIN_SEGMENTS)
    update = new_first / (jnp.sqrt(new_second) + 1e-06)
    update = jnp.where(position < big_end, update + 0.01 * weight_p, update)
    spans = [(packed_start[k], packed_start[k] + piece_len[k]) for k in range(11)]

    def span_of(block, a, b):
        if a % 128 == 0 and b % 128 == 0:
            return block[a // 128 : b // 128]
        return block[a // 128, a % 128 : (b - 1) % 128 + 1]

    sums = global_sums(
        [jnp.sum(jnp.square(span_of(weight_p, a, b))) for a, b in spans]
        + [jnp.sum(jnp.square(span_of(update, a, b))) for a, b in spans]
    )
    trust = jnp.sqrt(sums[0]) / jnp.sqrt(sums[1])
    scale = jnp.zeros((rows, 128), jnp.float32)
    for k in range(11):
        a, b = spans[k]
        scale = jnp.where((position >= a) & (position < b), trust[k], scale)
    new_weights = weight_p - 0.1 * scale * update
    rounded = new_weights.astype(jnp.bfloat16)
    gathered = lax.all_gather(rounded, "dp", axis=0, tiled=False)
    gathered = gathered.reshape(owners, padded)
    copies = [None] * 11
    for k in range(11):
        part = gathered[:, packed_start[k] : packed_start[k] + piece_len[k]]
        copies[k] = part.reshape(shapes[k])
    return (
        to_flat(new_weights),
        to_flat(new_first),
        to_flat(new_second),
        *copies,
    )


def solution(mesh):
    return jax.shard_map(
        on_device,
        mesh=mesh,
        in_specs=(
            P("dp", "tensor"),
            P("dp", None, "tensor"),
            P("dp", None, "tensor"),
            P("dp", None, "tensor"),
            P("dp", "tensor"),
            P("dp", None, "tensor"),
            P("dp", "tensor", None),
            P("dp", "tensor"),
            P("dp", None, "tensor"),
            P("dp", None, "tensor"),
            P("dp", "tensor", None),
            P("tensor", "dp"),
            P("tensor", "dp"),
            P("tensor", "dp"),
        ),
        out_specs=(
            P("tensor", "dp"),
            P("tensor", "dp"),
            P("tensor", "dp"),
            P("tensor"),
            P(None, "tensor"),
            P(None, "tensor"),
            P(None, "tensor"),
            P("tensor"),
            P(None, "tensor"),
            P("tensor", None),
            P("tensor"),
            P(None, "tensor"),
            P(None, "tensor"),
            P("tensor", None),
        ),
        check_vma=False,
    )
```

```python
import functools

import jax
import jax.numpy as jnp
from jax import lax
from jax.experimental import pallas as pl
from jax.experimental.pallas import tpu as pltpu
from jax.sharding import PartitionSpec as P

MESH = pl.DeviceIdType.MESH

GAIN_SEGMENTS = (0, 4, 7)


def norm_kernel(nd, nt, count, *refs):
    scalars = refs[:count]
    out_ref = refs[count]
    recv_a, recv_b, send_a, got_a, send_b, got_b = refs[count + 1 :]
    d = lax.axis_index("dp")
    t = lax.axis_index("tensor")
    barrier = pltpu.get_barrier_semaphore()
    for step in range(1, nt):
        pl.semaphore_signal(
            barrier, inc=1, device_id=(d, lax.rem(t + step, nt)), device_id_type=MESH
        )
    for step in range(1, nd):
        pl.semaphore_signal(
            barrier, inc=1, device_id=(lax.rem(d + step, nd), t), device_id_type=MESH
        )
    pl.semaphore_wait(barrier, nt - 1 + nd - 1)
    row = lax.broadcasted_iota(jnp.int32, (8, 128), 0)
    lane = lax.broadcasted_iota(jnp.int32, (8, 128), 1)
    half = count // 2
    vec = jnp.zeros((8, 128), jnp.float32)
    for k in range(count):
        hit = (row == k // half) & (lane == k % half)
        vec = jnp.where(hit, scalars[k][0, 0], vec)
    recv_a[t] = vec
    copies = []
    for step in range(1, nt):
        copy = pltpu.make_async_remote_copy(
            src_ref=recv_a.at[t],
            dst_ref=recv_a.at[t],
            send_sem=send_a.at[step],
            recv_sem=got_a.at[t],
            device_id=(d, lax.rem(t + step, nt)),
            device_id_type=MESH,
        )
        copy.start()
        copies.append(copy)
    for step in range(1, nt):
        source = lax.rem(t + nt - step, nt)
        pltpu.make_async_remote_copy(
            src_ref=recv_a.at[source],
            dst_ref=recv_a.at[source],
            send_sem=send_a.at[step],
            recv_sem=got_a.at[source],
            device_id=(d, source),
            device_id_type=MESH,
        ).wait_recv()
    for copy in copies:
        copy.wait_send()
    acc = recv_a[0]
    for slot in range(1, nt):
        acc = acc + recv_a[slot]
    recv_b[d] = acc
    copies = []
    for step in range(1, nd):
        copy = pltpu.make_async_remote_copy(
            src_ref=recv_b.at[d],
            dst_ref=recv_b.at[d],
            send_sem=send_b.at[step],
            recv_sem=got_b.at[d],
            device_id=(lax.rem(d + step, nd), t),
            device_id_type=MESH,
        )
        copy.start()
        copies.append(copy)
    for step in range(1, nd):
        source = lax.rem(d + nd - step, nd)
        pltpu.make_async_remote_copy(
            src_ref=recv_b.at[source],
            dst_ref=recv_b.at[source],
            send_sem=send_b.at[step],
            recv_sem=got_b.at[source],
            device_id=(source, t),
            device_id_type=MESH,
        ).wait_recv()
    for copy in copies:
        copy.wait_send()
    acc = recv_b[0]
    for slot in range(1, nd):
        acc = acc + recv_b[slot]
    out_ref[...] = acc


def global_sums(values):
    nd = lax.axis_size("dp")
    nt = lax.axis_size("tensor")
    count = len(values)
    return pl.pallas_call(
        functools.partial(norm_kernel, nd, nt, count),
        out_shape=jax.ShapeDtypeStruct((8, 128), jnp.float32),
        in_specs=[pl.BlockSpec(memory_space=pltpu.SMEM)] * count,
        out_specs=pl.BlockSpec(memory_space=pltpu.VMEM),
        scratch_shapes=[
            pltpu.VMEM((nt, 8, 128), jnp.float32),
            pltpu.VMEM((nd, 8, 128), jnp.float32),
            pltpu.SemaphoreType.DMA((nt,)),
            pltpu.SemaphoreType.DMA((nt,)),
            pltpu.SemaphoreType.DMA((nd,)),
            pltpu.SemaphoreType.DMA((nd,)),
        ],
        compiler_params=pltpu.CompilerParams(collective_id=0, has_side_effects=True),
    )(*[v.reshape(1, 1) for v in values])


def on_device(*args):
    grads = args[:11]
    weights, first_moment, second_moment = args[11:]
    owners = lax.axis_size("dp")
    shapes = [g.shape[1:] for g in grads]
    pieces = [g.reshape(owners, -1) for g in grads]
    piece_len = [p.shape[1] for p in pieces]
    starts = [sum(piece_len[:k]) for k in range(11)]
    own_count = sum(piece_len)
    order = [k for k in range(11) if k not in GAIN_SEGMENTS] + list(GAIN_SEGMENTS)
    packed_len = sum(piece_len)
    padded = -(-packed_len // 1024) * 1024
    rows = padded // 128
    blocks = [pieces[k].reshape(owners, -1, 128) for k in order if k not in GAIN_SEGMENTS]
    gains = jnp.concatenate([pieces[k] for k in GAIN_SEGMENTS], axis=1)
    gain_width = gains.shape[1]
    gains = jnp.pad(gains, ((0, 0), (0, 128 - gain_width))).reshape(owners, 1, 128)
    blocks.append(gains)
    used_rows = sum(b.shape[1] for b in blocks)
    blocks.append(jnp.zeros((owners, rows - used_rows, 128), gains.dtype))
    flat = jnp.concatenate(blocks, axis=1)
    summed = lax.psum_scatter(flat, "dp", scatter_dimension=0, tiled=True)
    summed = lax.optimization_barrier(summed).reshape(-1)
    packed_start = {}
    offset = 0
    for k in order:
        packed_start[k] = offset
        offset += piece_len[k]

    def to_packed(row):
        parts = [row[starts[k] : starts[k] + piece_len[k]] for k in order]
        parts.append(jnp.zeros((padded - packed_len,), row.dtype))
        return jnp.concatenate(parts).reshape(rows, 128)

    def to_flat(block):
        row = block.reshape(-1)
        parts = [row[packed_start[k] : packed_start[k] + piece_len[k]] for k in range(11)]
        return jnp.concatenate(parts).reshape(1, -1)

    grad = summed.reshape(rows, 128).astype(jnp.float32)
    weight_p = to_packed(weights.reshape(-1))
    first_p = to_packed(first_moment.reshape(-1))
    second_p = to_packed(second_moment.reshape(-1))
    new_first = 0.9 * first_p + 0.1 * grad
    new_second = 0.999 * second_p + 0.001 * grad * grad
    position = (
        lax.broadcasted_iota(jnp.int32, (rows, 128), 0) * 128
        + lax.broadcasted_iota(jnp.int32, (rows, 128), 1)
    )
    big_end = min(packed_start[k] for k in GAIN_SEGMENTS)
    update = new_first / (jnp.sqrt(new_second) + 1e-06)
    update = jnp.where(position < big_end, update + 0.01 * weight_p, update)
    update, new_first, new_second = lax.optimization_barrier((update, new_first, new_second))
    spans = [(packed_start[k], packed_start[k] + piece_len[k]) for k in range(11)]

    def span_of(block, a, b):
        if a % 128 == 0 and b % 128 == 0:
            return block[a // 128 : b // 128]
        return block[a // 128, a % 128 : (b - 1) % 128 + 1]

    sums = global_sums(
        [jnp.sum(jnp.square(span_of(weight_p, a, b))) for a, b in spans]
        + [jnp.sum(jnp.square(span_of(update, a, b))) for a, b in spans]
    )
    trust = jnp.sqrt(sums[0]) / jnp.sqrt(sums[1])
    row = lax.broadcasted_iota(jnp.int32, (rows, 128), 0)
    lane = lax.broadcasted_iota(jnp.int32, (rows, 128), 1)
    scale = jnp.zeros((rows, 128), jnp.float32)
    for k in reversed(order):
        a, b = spans[k]
        if a % 128 == 0 and b % 128 == 0:
            hit = row < b // 128
        else:
            hit = (row == a // 128) & (lane < (b - 1) % 128 + 1)
        scale = jnp.where(hit, trust[k], scale)
    new_weights = weight_p - 0.1 * scale * update
    rounded = new_weights.astype(jnp.bfloat16)
    gathered = lax.all_gather(rounded, "dp", axis=0, tiled=False)
    gathered = gathered.reshape(owners, padded)
    copies = [None] * 11
    for k in range(11):
        part = gathered[:, packed_start[k] : packed_start[k] + piece_len[k]]
        copies[k] = part.reshape(shapes[k])
    return (
        to_flat(new_weights),
        to_flat(new_first),
        to_flat(new_second),
        *copies,
    )


def solution(mesh):
    return jax.shard_map(
        on_device,
        mesh=mesh,
        in_specs=(
            P("dp", "tensor"),
            P("dp", None, "tensor"),
            P("dp", None, "tensor"),
            P("dp", None, "tensor"),
            P("dp", "tensor"),
            P("dp", None, "tensor"),
            P("dp", "tensor", None),
            P("dp", "tensor"),
            P("dp", None, "tensor"),
            P("dp", None, "tensor"),
            P("dp", "tensor", None),
            P("tensor", "dp"),
            P("tensor", "dp"),
            P("tensor", "dp"),
        ),
        out_specs=(
            P("tensor", "dp"),
            P("tensor", "dp"),
            P("tensor", "dp"),
            P("tensor"),
            P(None, "tensor"),
            P(None, "tensor"),
            P(None, "tensor"),
            P("tensor"),
            P(None, "tensor"),
            P("tensor", None),
            P("tensor"),
            P(None, "tensor"),
            P(None, "tensor"),
            P("tensor", None),
        ),
        check_vma=False,
    )
```

```python
import functools

import jax
import jax.numpy as jnp
from jax import lax
from jax.experimental import pallas as pl
from jax.experimental.pallas import tpu as pltpu
from jax.sharding import PartitionSpec as P

MESH = pl.DeviceIdType.MESH

GAIN_SEGMENTS = (0, 4, 7)


def apply_kernel(nd, nt, segments, weight_ref, update_ref, new_ref, low_ref, *scratch):
    recv_a, recv_b, send_a, got_a, send_b, got_b = scratch
    d = lax.axis_index("dp")
    t = lax.axis_index("tensor")
    barrier = pltpu.get_barrier_semaphore()
    for step in range(1, nt):
        pl.semaphore_signal(
            barrier, inc=1, device_id=(d, lax.rem(t + step, nt)), device_id_type=MESH
        )
    for step in range(1, nd):
        pl.semaphore_signal(
            barrier, inc=1, device_id=(lax.rem(d + step, nd), t), device_id_type=MESH
        )
    row = lax.broadcasted_iota(jnp.int32, (8, 128), 0)
    lane = lax.broadcasted_iota(jnp.int32, (8, 128), 1)

    def total(x):
        return jnp.sum(jnp.sum(x, axis=0, keepdims=True), axis=1, keepdims=True)

    def pick(vec, k):
        return total(jnp.where((row == 0) & (lane == k), vec, 0.0))

    vec = jnp.zeros((8, 128), jnp.float32)
    for k, (r0, r1, l0, l1) in enumerate(segments):
        if l0 is None:
            acc_w = jnp.zeros((8, 128), jnp.float32)
            acc_u = jnp.zeros((8, 128), jnp.float32)
            for r in range(r0, r1, 32):
                w = weight_ref[r : r + 32, :]
                u = update_ref[r : r + 32, :]
                acc_w = acc_w + jnp.sum((w * w).reshape(4, 8, 128), axis=0)
                acc_u = acc_u + jnp.sum((u * u).reshape(4, 8, 128), axis=0)
        else:
            keep = (row == 0) & (lane >= l0) & (lane < l1)
            w = weight_ref[r0 : r0 + 8, :]
            u = update_ref[r0 : r0 + 8, :]
            acc_w = jnp.where(keep, w * w, 0.0)
            acc_u = jnp.where(keep, u * u, 0.0)
        vec = jnp.where((row == 0) & (lane == k), total(acc_w), vec)
        vec = jnp.where((row == 1) & (lane == k), total(acc_u), vec)
    pl.semaphore_wait(barrier, nt - 1 + nd - 1)
    recv_a[t] = vec
    copies = []
    for step in range(1, nt):
        copy = pltpu.make_async_remote_copy(
            src_ref=recv_a.at[t],
            dst_ref=recv_a.at[t],
            send_sem=send_a.at[step],
            recv_sem=got_a.at[t],
            device_id=(d, lax.rem(t + step, nt)),
            device_id_type=MESH,
        )
        copy.start()
        copies.append(copy)
    for step in range(1, nt):
        source = lax.rem(t + nt - step, nt)
        pltpu.make_async_remote_copy(
            src_ref=recv_a.at[source],
            dst_ref=recv_a.at[source],
            send_sem=send_a.at[step],
            recv_sem=got_a.at[source],
            device_id=(d, source),
            device_id_type=MESH,
        ).wait_recv()
    for copy in copies:
        copy.wait_send()
    acc = recv_a[0]
    for slot in range(1, nt):
        acc = acc + recv_a[slot]
    recv_b[d] = acc
    copies = []
    for step in range(1, nd):
        copy = pltpu.make_async_remote_copy(
            src_ref=recv_b.at[d],
            dst_ref=recv_b.at[d],
            send_sem=send_b.at[step],
            recv_sem=got_b.at[d],
            device_id=(lax.rem(d + step, nd), t),
            device_id_type=MESH,
        )
        copy.start()
        copies.append(copy)
    for step in range(1, nd):
        source = lax.rem(d + nd - step, nd)
        pltpu.make_async_remote_copy(
            src_ref=recv_b.at[source],
            dst_ref=recv_b.at[source],
            send_sem=send_b.at[step],
            recv_sem=got_b.at[source],
            device_id=(source, t),
            device_id_type=MESH,
        ).wait_recv()
    for copy in copies:
        copy.wait_send()
    acc = recv_b[0]
    for slot in range(1, nd):
        acc = acc + recv_b[slot]
    trust = jnp.sqrt(acc[0:1, :]) / jnp.sqrt(acc[1:2, :])
    trust = jnp.broadcast_to(trust, (8, 128))
    gain_scale = jnp.zeros((8, 128), jnp.float32)
    for k, (r0, r1, l0, l1) in enumerate(segments):
        factor = 0.1 * pick(trust, k)
        if l0 is None:
            for r in range(r0, r1, 32):
                w = weight_ref[r : r + 32, :]
                u = update_ref[r : r + 32, :]
                new = w - factor * u
                new_ref[r : r + 32, :] = new
                low_ref[r : r + 32, :] = new.astype(low_ref.dtype)
        else:
            gain_scale = jnp.where((lane >= l0) & (lane < l1), factor, gain_scale)
            tail = r0
    for r in range(tail, weight_ref.shape[0], 8):
        w = weight_ref[r : r + 8, :]
        u = update_ref[r : r + 8, :]
        scale = gain_scale if r == tail else jnp.zeros((8, 128), jnp.float32)
        new = w - scale * u
        new_ref[r : r + 8, :] = new
        low_ref[r : r + 8, :] = new.astype(low_ref.dtype)


def apply_step(weight_p, update, segments):
    nd = lax.axis_size("dp")
    nt = lax.axis_size("tensor")
    return pl.pallas_call(
        functools.partial(apply_kernel, nd, nt, segments),
        out_shape=(
            jax.ShapeDtypeStruct(weight_p.shape, jnp.float32),
            jax.ShapeDtypeStruct(weight_p.shape, jnp.bfloat16),
        ),
        in_specs=[pl.BlockSpec(memory_space=pltpu.VMEM)] * 2,
        out_specs=(
            pl.BlockSpec(memory_space=pltpu.VMEM),
            pl.BlockSpec(memory_space=pltpu.VMEM),
        ),
        scratch_shapes=[
            pltpu.VMEM((nt, 8, 128), jnp.float32),
            pltpu.VMEM((nd, 8, 128), jnp.float32),
            pltpu.SemaphoreType.DMA((nt,)),
            pltpu.SemaphoreType.DMA((nt,)),
            pltpu.SemaphoreType.DMA((nd,)),
            pltpu.SemaphoreType.DMA((nd,)),
        ],
        compiler_params=pltpu.CompilerParams(collective_id=0, has_side_effects=True),
    )(weight_p, update)


def on_device(*args):
    grads = args[:11]
    weights, first_moment, second_moment = args[11:]
    owners = lax.axis_size("dp")
    shapes = [g.shape[1:] for g in grads]
    pieces = [g.reshape(owners, -1) for g in grads]
    piece_len = [p.shape[1] for p in pieces]
    starts = [sum(piece_len[:k]) for k in range(11)]
    own_count = sum(piece_len)
    order = [k for k in range(11) if k not in GAIN_SEGMENTS] + list(GAIN_SEGMENTS)
    packed_len = sum(piece_len)
    padded = -(-packed_len // 1024) * 1024
    pad = jnp.zeros((owners, padded - packed_len), grads[0].dtype)
    flat = jnp.concatenate([pieces[k] for k in order] + [pad], axis=1)
    flat = flat.reshape(owners, padded // 128, 128)
    summed = lax.psum_scatter(flat, "dp", scatter_dimension=0, tiled=True)
    summed = lax.optimization_barrier(summed).reshape(-1)
    packed_start = {}
    offset = 0
    for k in order:
        packed_start[k] = offset
        offset += piece_len[k]
    rows = padded // 128

    def to_packed(row):
        parts = [row[starts[k] : starts[k] + piece_len[k]] for k in order]
        parts.append(jnp.zeros((padded - packed_len,), row.dtype))
        return jnp.concatenate(parts).reshape(rows, 128)

    def to_flat(block):
        row = block.reshape(-1)
        parts = [row[packed_start[k] : packed_start[k] + piece_len[k]] for k in range(11)]
        return jnp.concatenate(parts).reshape(1, -1)

    grad = summed.reshape(rows, 128).astype(jnp.float32)
    weight_p = to_packed(weights.reshape(-1))
    first_p = to_packed(first_moment.reshape(-1))
    second_p = to_packed(second_moment.reshape(-1))
    new_first = 0.9 * first_p + 0.1 * grad
    new_second = 0.999 * second_p + 0.001 * grad * grad
    position = (
        lax.broadcasted_iota(jnp.int32, (rows, 128), 0) * 128
        + lax.broadcasted_iota(jnp.int32, (rows, 128), 1)
    )
    big_end = min(packed_start[k] for k in GAIN_SEGMENTS)
    update = new_first / (jnp.sqrt(new_second) + 1e-06)
    update = jnp.where(position < big_end, update + 0.01 * weight_p, update)
    segments = []
    for k in range(11):
        a, b = packed_start[k], packed_start[k] + piece_len[k]
        if a % 128 == 0 and b % 128 == 0:
            segments.append((a // 128, b // 128, None, None))
        else:
            segments.append((a // 128, a // 128 + 1, a % 128, (b - 1) % 128 + 1))
    new_weights, rounded = apply_step(weight_p, update, tuple(segments))
    gathered = lax.all_gather(rounded, "dp", axis=0, tiled=False)
    gathered = gathered.reshape(owners, padded)
    copies = [None] * 11
    for k in range(11):
        part = gathered[:, packed_start[k] : packed_start[k] + piece_len[k]]
        copies[k] = part.reshape(shapes[k])
    return (
        to_flat(new_weights),
        to_flat(new_first),
        to_flat(new_second),
        *copies,
    )


def solution(mesh):
    return jax.shard_map(
        on_device,
        mesh=mesh,
        in_specs=(
            P("dp", "tensor"),
            P("dp", None, "tensor"),
            P("dp", None, "tensor"),
            P("dp", None, "tensor"),
            P("dp", "tensor"),
            P("dp", None, "tensor"),
            P("dp", "tensor", None),
            P("dp", "tensor"),
            P("dp", None, "tensor"),
            P("dp", None, "tensor"),
            P("dp", "tensor", None),
            P("tensor", "dp"),
            P("tensor", "dp"),
            P("tensor", "dp"),
        ),
        out_specs=(
            P("tensor", "dp"),
            P("tensor", "dp"),
            P("tensor", "dp"),
            P("tensor"),
            P(None, "tensor"),
            P(None, "tensor"),
            P(None, "tensor"),
            P("tensor"),
            P(None, "tensor"),
            P("tensor", None),
            P("tensor"),
            P(None, "tensor"),
            P(None, "tensor"),
            P("tensor", None),
        ),
        check_vma=False,
    )
```

```python
import functools

import jax
import jax.numpy as jnp
from jax import lax
from jax.experimental import pallas as pl
from jax.experimental.pallas import tpu as pltpu
from jax.sharding import PartitionSpec as P

MESH = pl.DeviceIdType.MESH

GAIN_SEGMENTS = (0, 4, 7)


def apply_kernel(nd, nt, segments, weight_ref, update_ref, new_ref, low_ref, *scratch):
    recv_a, recv_b, send_a, got_a, send_b, got_b = scratch
    d = lax.axis_index("dp")
    t = lax.axis_index("tensor")
    barrier = pltpu.get_barrier_semaphore()
    for step in range(1, nt):
        pl.semaphore_signal(
            barrier, inc=1, device_id=(d, lax.rem(t + step, nt)), device_id_type=MESH
        )
    for step in range(1, nd):
        pl.semaphore_signal(
            barrier, inc=1, device_id=(lax.rem(d + step, nd), t), device_id_type=MESH
        )
    row = lax.broadcasted_iota(jnp.int32, (8, 128), 0)
    lane = lax.broadcasted_iota(jnp.int32, (8, 128), 1)

    def total(x):
        return jnp.sum(jnp.sum(x, axis=0, keepdims=True), axis=1, keepdims=True)

    def pick(vec, k):
        return total(jnp.where((row == 0) & (lane == k), vec, 0.0))

    vec = jnp.zeros((8, 128), jnp.float32)
    for k, (r0, r1, l0, l1) in enumerate(segments):
        if l0 is None:
            acc_w = jnp.zeros((8, 128), jnp.float32)
            acc_u = jnp.zeros((8, 128), jnp.float32)
            for r in range(r0, r1, 32):
                w = weight_ref[r : r + 32, :]
                u = update_ref[r : r + 32, :]
                acc_w = acc_w + jnp.sum((w * w).reshape(4, 8, 128), axis=0)
                acc_u = acc_u + jnp.sum((u * u).reshape(4, 8, 128), axis=0)
        else:
            keep = (row == 0) & (lane >= l0) & (lane < l1)
            w = weight_ref[r0 : r0 + 8, :]
            u = update_ref[r0 : r0 + 8, :]
            acc_w = jnp.where(keep, w * w, 0.0)
            acc_u = jnp.where(keep, u * u, 0.0)
        vec = jnp.where((row == 0) & (lane == k), total(acc_w), vec)
        vec = jnp.where((row == 1) & (lane == k), total(acc_u), vec)
    pl.semaphore_wait(barrier, nt - 1 + nd - 1)
    recv_a[t] = vec
    copies = []
    for step in range(1, nt):
        copy = pltpu.make_async_remote_copy(
            src_ref=recv_a.at[t],
            dst_ref=recv_a.at[t],
            send_sem=send_a.at[step],
            recv_sem=got_a.at[t],
            device_id=(d, lax.rem(t + step, nt)),
            device_id_type=MESH,
        )
        copy.start()
        copies.append(copy)
    for step in range(1, nt):
        source = lax.rem(t + nt - step, nt)
        pltpu.make_async_remote_copy(
            src_ref=recv_a.at[source],
            dst_ref=recv_a.at[source],
            send_sem=send_a.at[step],
            recv_sem=got_a.at[source],
            device_id=(d, source),
            device_id_type=MESH,
        ).wait_recv()
    for copy in copies:
        copy.wait_send()
    acc = recv_a[0]
    for slot in range(1, nt):
        acc = acc + recv_a[slot]
    recv_b[d] = acc
    copies = []
    for step in range(1, nd):
        copy = pltpu.make_async_remote_copy(
            src_ref=recv_b.at[d],
            dst_ref=recv_b.at[d],
            send_sem=send_b.at[step],
            recv_sem=got_b.at[d],
            device_id=(lax.rem(d + step, nd), t),
            device_id_type=MESH,
        )
        copy.start()
        copies.append(copy)
    for step in range(1, nd):
        source = lax.rem(d + nd - step, nd)
        pltpu.make_async_remote_copy(
            src_ref=recv_b.at[source],
            dst_ref=recv_b.at[source],
            send_sem=send_b.at[step],
            recv_sem=got_b.at[source],
            device_id=(source, t),
            device_id_type=MESH,
        ).wait_recv()
    for copy in copies:
        copy.wait_send()
    acc = recv_b[0]
    for slot in range(1, nd):
        acc = acc + recv_b[slot]
    trust = jnp.sqrt(acc[0:1, :]) / jnp.sqrt(acc[1:2, :])
    trust = jnp.broadcast_to(trust, (8, 128))
    gain_scale = jnp.zeros((8, 128), jnp.float32)
    for k, (r0, r1, l0, l1) in enumerate(segments):
        factor = 0.1 * pick(trust, k)
        if l0 is None:
            for r in range(r0, r1, 32):
                w = weight_ref[r : r + 32, :]
                u = update_ref[r : r + 32, :]
                new = w - factor * u
                new_ref[r : r + 32, :] = new
                low_ref[r : r + 32, :] = new.astype(low_ref.dtype)
        else:
            gain_scale = jnp.where((lane >= l0) & (lane < l1), factor, gain_scale)
            tail = r0
    for r in range(tail, weight_ref.shape[0], 8):
        w = weight_ref[r : r + 8, :]
        u = update_ref[r : r + 8, :]
        scale = gain_scale if r == tail else jnp.zeros((8, 128), jnp.float32)
        new = w - scale * u
        new_ref[r : r + 8, :] = new
        low_ref[r : r + 8, :] = new.astype(low_ref.dtype)


def apply_step(weight_p, update, segments):
    nd = lax.axis_size("dp")
    nt = lax.axis_size("tensor")
    return pl.pallas_call(
        functools.partial(apply_kernel, nd, nt, segments),
        out_shape=(
            jax.ShapeDtypeStruct(weight_p.shape, jnp.float32),
            jax.ShapeDtypeStruct(weight_p.shape, jnp.bfloat16),
        ),
        in_specs=[pl.BlockSpec(memory_space=pltpu.VMEM)] * 2,
        out_specs=(
            pl.BlockSpec(memory_space=pltpu.VMEM),
            pl.BlockSpec(memory_space=pltpu.VMEM),
        ),
        scratch_shapes=[
            pltpu.VMEM((nt, 8, 128), jnp.float32),
            pltpu.VMEM((nd, 8, 128), jnp.float32),
            pltpu.SemaphoreType.DMA((nt,)),
            pltpu.SemaphoreType.DMA((nt,)),
            pltpu.SemaphoreType.DMA((nd,)),
            pltpu.SemaphoreType.DMA((nd,)),
        ],
        compiler_params=pltpu.CompilerParams(collective_id=0, has_side_effects=True),
    )(weight_p, update)


def on_device(*args):
    grads = args[:11]
    weights, first_moment, second_moment = args[11:]
    owners = lax.axis_size("dp")
    shapes = [g.shape[1:] for g in grads]
    pieces = [g.reshape(owners, -1) for g in grads]
    piece_len = [p.shape[1] for p in pieces]
    starts = [sum(piece_len[:k]) for k in range(11)]
    own_count = sum(piece_len)
    order = [k for k in range(11) if k not in GAIN_SEGMENTS] + list(GAIN_SEGMENTS)
    packed_len = sum(piece_len)
    padded = -(-packed_len // 1024) * 1024
    pad = jnp.zeros((owners, padded - packed_len), grads[0].dtype)
    flat = jnp.concatenate([pieces[k] for k in order] + [pad], axis=1)
    flat = flat.reshape(owners, padded // 128, 128)
    summed = lax.psum_scatter(flat, "dp", scatter_dimension=0, tiled=True)
    summed = lax.optimization_barrier(summed).reshape(-1)
    packed_start = {}
    offset = 0
    for k in order:
        packed_start[k] = offset
        offset += piece_len[k]
    rows = padded // 128

    def to_packed(row):
        parts = [row[starts[k] : starts[k] + piece_len[k]] for k in order]
        parts.append(jnp.zeros((padded - packed_len,), row.dtype))
        return jnp.concatenate(parts).reshape(rows, 128)

    def to_flat(block):
        row = block.reshape(-1)
        parts = [row[packed_start[k] : packed_start[k] + piece_len[k]] for k in range(11)]
        return jnp.concatenate(parts).reshape(1, -1)

    grad = summed.reshape(rows, 128).astype(jnp.float32)
    weight_p = to_packed(weights.reshape(-1))
    first_p = to_packed(first_moment.reshape(-1))
    second_p = to_packed(second_moment.reshape(-1))
    new_first = 0.9 * first_p + 0.1 * grad
    new_second = 0.999 * second_p + 0.001 * grad * grad
    position = (
        lax.broadcasted_iota(jnp.int32, (rows, 128), 0) * 128
        + lax.broadcasted_iota(jnp.int32, (rows, 128), 1)
    )
    big_end = min(packed_start[k] for k in GAIN_SEGMENTS)
    update = new_first / (jnp.sqrt(new_second) + 1e-06)
    update = jnp.where(position < big_end, update + 0.01 * weight_p, update)
    segments = []
    for k in range(11):
        a, b = packed_start[k], packed_start[k] + piece_len[k]
        if a % 128 == 0 and b % 128 == 0:
            segments.append((a // 128, b // 128, None, None))
        else:
            segments.append((a // 128, a // 128 + 1, a % 128, (b - 1) % 128 + 1))
    new_weights, rounded = apply_step(weight_p, update, tuple(segments))
    gathered = lax.all_gather(rounded, "dp", axis=0, tiled=False)
    copies = [None] * 11
    for k in range(11):
        r0, r1, l0, l1 = segments[k]
        if l0 is None:
            part = gathered[:, r0:r1, :]
        else:
            part = gathered[:, r0, l0:l1]
        copies[k] = part.reshape(shapes[k])
    return (
        to_flat(new_weights),
        to_flat(new_first),
        to_flat(new_second),
        *copies,
    )


def solution(mesh):
    return jax.shard_map(
        on_device,
        mesh=mesh,
        in_specs=(
            P("dp", "tensor"),
            P("dp", None, "tensor"),
            P("dp", None, "tensor"),
            P("dp", None, "tensor"),
            P("dp", "tensor"),
            P("dp", None, "tensor"),
            P("dp", "tensor", None),
            P("dp", "tensor"),
            P("dp", None, "tensor"),
            P("dp", None, "tensor"),
            P("dp", "tensor", None),
            P("tensor", "dp"),
            P("tensor", "dp"),
            P("tensor", "dp"),
        ),
        out_specs=(
            P("tensor", "dp"),
            P("tensor", "dp"),
            P("tensor", "dp"),
            P("tensor"),
            P(None, "tensor"),
            P(None, "tensor"),
            P(None, "tensor"),
            P("tensor"),
            P(None, "tensor"),
            P("tensor", None),
            P("tensor"),
            P(None, "tensor"),
            P(None, "tensor"),
            P("tensor", None),
        ),
        check_vma=False,
    )
```

```python
import functools

import jax
import jax.numpy as jnp
from jax import lax
from jax.experimental import pallas as pl
from jax.experimental.pallas import tpu as pltpu
from jax.sharding import PartitionSpec as P

MESH = pl.DeviceIdType.MESH

GAIN_SEGMENTS = (0, 4, 7)


def apply_kernel(nd, nt, segments, weight_ref, update_ref, new_ref, low_ref, *scratch):
    recv_a, recv_b, send_a, got_a, send_b, got_b = scratch
    d = lax.axis_index("dp")
    t = lax.axis_index("tensor")
    barrier = pltpu.get_barrier_semaphore()
    for step in range(1, nt):
        pl.semaphore_signal(
            barrier, inc=1, device_id=(d, lax.rem(t + step, nt)), device_id_type=MESH
        )
    for step in range(1, nd):
        pl.semaphore_signal(
            barrier, inc=1, device_id=(lax.rem(d + step, nd), t), device_id_type=MESH
        )
    row = lax.broadcasted_iota(jnp.int32, (8, 128), 0)
    lane = lax.broadcasted_iota(jnp.int32, (8, 128), 1)

    def total(x):
        return jnp.sum(jnp.sum(x, axis=0, keepdims=True), axis=1, keepdims=True)

    def pick(vec, k):
        return total(jnp.where((row == 0) & (lane == k), vec, 0.0))

    vec = jnp.zeros((8, 128), jnp.float32)
    for k, (r0, r1, l0, l1) in enumerate(segments):
        if l0 is None:
            acc_w = jnp.zeros((8, 128), jnp.float32)
            acc_u = jnp.zeros((8, 128), jnp.float32)
            for r in range(r0, r1, 32):
                w = weight_ref[r : r + 32, :]
                u = update_ref[r : r + 32, :]
                acc_w = acc_w + jnp.sum((w * w).reshape(4, 8, 128), axis=0)
                acc_u = acc_u + jnp.sum((u * u).reshape(4, 8, 128), axis=0)
        else:
            keep = (row == 0) & (lane >= l0) & (lane < l1)
            w = weight_ref[r0 : r0 + 8, :]
            u = update_ref[r0 : r0 + 8, :]
            acc_w = jnp.where(keep, w * w, 0.0)
            acc_u = jnp.where(keep, u * u, 0.0)
        vec = jnp.where((row == 0) & (lane == k), total(acc_w), vec)
        vec = jnp.where((row == 1) & (lane == k), total(acc_u), vec)
    pl.semaphore_wait(barrier, nt - 1 + nd - 1)
    recv_a[t] = vec
    copies = []
    for step in range(1, nt):
        copy = pltpu.make_async_remote_copy(
            src_ref=recv_a.at[t],
            dst_ref=recv_a.at[t],
            send_sem=send_a.at[step],
            recv_sem=got_a.at[t],
            device_id=(d, lax.rem(t + step, nt)),
            device_id_type=MESH,
        )
        copy.start()
        copies.append(copy)
    for step in range(1, nt):
        source = lax.rem(t + nt - step, nt)
        pltpu.make_async_remote_copy(
            src_ref=recv_a.at[source],
            dst_ref=recv_a.at[source],
            send_sem=send_a.at[step],
            recv_sem=got_a.at[source],
            device_id=(d, source),
            device_id_type=MESH,
        ).wait_recv()
    for copy in copies:
        copy.wait_send()
    acc = recv_a[0]
    for slot in range(1, nt):
        acc = acc + recv_a[slot]
    recv_b[d] = acc
    copies = []
    for step in range(1, nd):
        copy = pltpu.make_async_remote_copy(
            src_ref=recv_b.at[d],
            dst_ref=recv_b.at[d],
            send_sem=send_b.at[step],
            recv_sem=got_b.at[d],
            device_id=(lax.rem(d + step, nd), t),
            device_id_type=MESH,
        )
        copy.start()
        copies.append(copy)
    for step in range(1, nd):
        source = lax.rem(d + nd - step, nd)
        pltpu.make_async_remote_copy(
            src_ref=recv_b.at[source],
            dst_ref=recv_b.at[source],
            send_sem=send_b.at[step],
            recv_sem=got_b.at[source],
            device_id=(source, t),
            device_id_type=MESH,
        ).wait_recv()
    for copy in copies:
        copy.wait_send()
    acc = recv_b[0]
    for slot in range(1, nd):
        acc = acc + recv_b[slot]
    trust = jnp.sqrt(acc[0:1, :]) / jnp.sqrt(acc[1:2, :])
    trust = jnp.broadcast_to(trust, (8, 128))
    gain_scale = jnp.zeros((8, 128), jnp.float32)
    for k, (r0, r1, l0, l1) in enumerate(segments):
        factor = 0.1 * pick(trust, k)
        if l0 is None:
            for r in range(r0, r1, 32):
                w = weight_ref[r : r + 32, :]
                u = update_ref[r : r + 32, :]
                new = w - factor * u
                new_ref[r : r + 32, :] = new
                low_ref[r : r + 32, :] = new.astype(low_ref.dtype)
        else:
            gain_scale = jnp.where((lane >= l0) & (lane < l1), factor, gain_scale)
            tail = r0
    for r in range(tail, weight_ref.shape[0], 8):
        w = weight_ref[r : r + 8, :]
        u = update_ref[r : r + 8, :]
        scale = gain_scale if r == tail else jnp.zeros((8, 128), jnp.float32)
        new = w - scale * u
        new_ref[r : r + 8, :] = new
        low_ref[r : r + 8, :] = new.astype(low_ref.dtype)


def apply_step(weight_p, update, segments):
    nd = lax.axis_size("dp")
    nt = lax.axis_size("tensor")
    return pl.pallas_call(
        functools.partial(apply_kernel, nd, nt, segments),
        out_shape=(
            jax.ShapeDtypeStruct(weight_p.shape, jnp.float32),
            jax.ShapeDtypeStruct(weight_p.shape, jnp.bfloat16),
        ),
        in_specs=[pl.BlockSpec(memory_space=pltpu.VMEM)] * 2,
        out_specs=(
            pl.BlockSpec(memory_space=pltpu.VMEM),
            pl.BlockSpec(memory_space=pltpu.VMEM),
        ),
        scratch_shapes=[
            pltpu.VMEM((nt, 8, 128), jnp.float32),
            pltpu.VMEM((nd, 8, 128), jnp.float32),
            pltpu.SemaphoreType.DMA((nt,)),
            pltpu.SemaphoreType.DMA((nt,)),
            pltpu.SemaphoreType.DMA((nd,)),
            pltpu.SemaphoreType.DMA((nd,)),
        ],
        compiler_params=pltpu.CompilerParams(collective_id=0, has_side_effects=True),
    )(weight_p, update)


def on_device(*args):
    grads = args[:11]
    weights, first_moment, second_moment = args[11:]
    owners = lax.axis_size("dp")
    shapes = [g.shape[1:] for g in grads]
    pieces = [g.reshape(owners, -1) for g in grads]
    piece_len = [p.shape[1] for p in pieces]
    starts = [sum(piece_len[:k]) for k in range(11)]
    order = [k for k in range(11) if k not in GAIN_SEGMENTS] + list(GAIN_SEGMENTS)
    packed_len = sum(piece_len)
    padded = -(-packed_len // 1024) * 1024
    rows = padded // 128
    blocks = [(g.shape[1] // owners, g.shape[2]) if g.ndim == 3 else None for g in grads]

    def to_rows(x, a, b):
        lead = x.shape[0]
        if a % 8 == 0 and b % 128 == 0:
            x = x.reshape(lead, a // 8, 8, b // 128, 128).transpose(0, 1, 3, 2, 4)
            return x.reshape(lead, a * b // 128, 128)
        if b % 128 != 0 and a == 128:
            return x.transpose(0, 2, 1)
        return x.reshape(lead, a * b // 128, 128)

    def from_rows(y, a, b):
        lead = y.shape[0]
        if a % 8 == 0 and b % 128 == 0:
            y = y.reshape(lead, a // 8, b // 128, 8, 128).transpose(0, 1, 3, 2, 4)
            return y.reshape(lead, a, b)
        if b % 128 != 0 and a == 128:
            return y.transpose(0, 2, 1)
        return y.reshape(lead, a, b)

    big = [k for k in order if k not in GAIN_SEGMENTS]
    parts = [to_rows(grads[k][0].reshape((owners,) + blocks[k]), *blocks[k]) for k in big]
    gains = jnp.concatenate([pieces[k] for k in GAIN_SEGMENTS], axis=1)
    gain_width = gains.shape[1]
    parts.append(jnp.pad(gains, ((0, 0), (0, 128 - gain_width))).reshape(owners, 1, 128))
    used_rows = sum(p.shape[1] for p in parts)
    parts.append(jnp.zeros((owners, rows - used_rows, 128), gains.dtype))
    flat = jnp.concatenate(parts, axis=1)
    summed = lax.psum_scatter(flat, "dp", scatter_dimension=0, tiled=True)
    summed = lax.optimization_barrier(summed).reshape(-1)
    packed_start = {}
    offset = 0
    for k in order:
        packed_start[k] = offset
        offset += piece_len[k]
    segments = []
    for k in range(11):
        a, b = packed_start[k], packed_start[k] + piece_len[k]
        if a % 128 == 0 and b % 128 == 0:
            segments.append((a // 128, b // 128, None, None))
        else:
            segments.append((a // 128, a // 128 + 1, a % 128, (b - 1) % 128 + 1))

    def to_packed(row):
        out = []
        for k in big:
            seg = row[starts[k] : starts[k] + piece_len[k]].reshape((1,) + blocks[k])
            out.append(to_rows(seg, *blocks[k])[0])
        tail = [row[starts[k] : starts[k] + piece_len[k]] for k in GAIN_SEGMENTS]
        tail.append(jnp.zeros((128 - gain_width,), row.dtype))
        out.append(jnp.concatenate(tail).reshape(1, 128))
        out.append(jnp.zeros((rows - used_rows, 128), row.dtype))
        return jnp.concatenate(out, axis=0)

    def to_flat(block):
        out = []
        for k in range(11):
            r0, r1, l0, l1 = segments[k]
            if l0 is None:
                seg = from_rows(block[r0:r1].reshape(1, r1 - r0, 128), *blocks[k])
                out.append(seg.reshape(-1))
            else:
                out.append(block[r0, l0:l1])
        return jnp.concatenate(out).reshape(1, -1)

    grad = summed.reshape(rows, 128).astype(jnp.float32)
    weight_p = to_packed(weights.reshape(-1))
    first_p = to_packed(first_moment.reshape(-1))
    second_p = to_packed(second_moment.reshape(-1))
    new_first = 0.9 * first_p + 0.1 * grad
    new_second = 0.999 * second_p + 0.001 * grad * grad
    position = (
        lax.broadcasted_iota(jnp.int32, (rows, 128), 0) * 128
        + lax.broadcasted_iota(jnp.int32, (rows, 128), 1)
    )
    big_end = min(packed_start[k] for k in GAIN_SEGMENTS)
    update = new_first / (jnp.sqrt(new_second) + 1e-06)
    update = jnp.where(position < big_end, update + 0.01 * weight_p, update)
    new_weights, rounded = apply_step(weight_p, update, tuple(segments))
    gathered = lax.all_gather(rounded, "dp", axis=0, tiled=False)
    copies = [None] * 11
    for k in range(11):
        r0, r1, l0, l1 = segments[k]
        if l0 is None:
            part = from_rows(gathered[:, r0:r1, :], *blocks[k])
        else:
            part = gathered[:, r0, l0:l1]
        copies[k] = part.reshape(shapes[k])
    return (
        to_flat(new_weights),
        to_flat(new_first),
        to_flat(new_second),
        *copies,
    )


def solution(mesh):
    return jax.shard_map(
        on_device,
        mesh=mesh,
        in_specs=(
            P("dp", "tensor"),
            P("dp", None, "tensor"),
            P("dp", None, "tensor"),
            P("dp", None, "tensor"),
            P("dp", "tensor"),
            P("dp", None, "tensor"),
            P("dp", "tensor", None),
            P("dp", "tensor"),
            P("dp", None, "tensor"),
            P("dp", None, "tensor"),
            P("dp", "tensor", None),
            P("tensor", "dp"),
            P("tensor", "dp"),
            P("tensor", "dp"),
        ),
        out_specs=(
            P("tensor", "dp"),
            P("tensor", "dp"),
            P("tensor", "dp"),
            P("tensor"),
            P(None, "tensor"),
            P(None, "tensor"),
            P(None, "tensor"),
            P("tensor"),
            P(None, "tensor"),
            P("tensor", None),
            P("tensor"),
            P(None, "tensor"),
            P(None, "tensor"),
            P("tensor", None),
        ),
        check_vma=False,
    )
```

```python
import functools

import jax
import jax.numpy as jnp
from jax import lax
from jax.experimental import pallas as pl
from jax.experimental.pallas import tpu as pltpu
from jax.experimental.layout import Layout, with_layout_constraint
from jax.sharding import PartitionSpec as P

MESH = pl.DeviceIdType.MESH

GAIN_SEGMENTS = (0, 4, 7)


def apply_kernel(nd, nt, segments, weight_ref, update_ref, new_ref, low_ref, *scratch):
    recv_a, recv_b, send_a, got_a, send_b, got_b = scratch
    d = lax.axis_index("dp")
    t = lax.axis_index("tensor")
    barrier = pltpu.get_barrier_semaphore()
    for step in range(1, nt):
        pl.semaphore_signal(
            barrier, inc=1, device_id=(d, lax.rem(t + step, nt)), device_id_type=MESH
        )
    for step in range(1, nd):
        pl.semaphore_signal(
            barrier, inc=1, device_id=(lax.rem(d + step, nd), t), device_id_type=MESH
        )
    row = lax.broadcasted_iota(jnp.int32, (8, 128), 0)
    lane = lax.broadcasted_iota(jnp.int32, (8, 128), 1)

    def total(x):
        return jnp.sum(jnp.sum(x, axis=0, keepdims=True), axis=1, keepdims=True)

    def pick(vec, k):
        return total(jnp.where((row == 0) & (lane == k), vec, 0.0))

    vec = jnp.zeros((8, 128), jnp.float32)
    for k, (r0, r1, l0, l1) in enumerate(segments):
        if l0 is None:
            acc_w = jnp.zeros((8, 128), jnp.float32)
            acc_u = jnp.zeros((8, 128), jnp.float32)
            for r in range(r0, r1, 32):
                w = weight_ref[r : r + 32, :]
                u = update_ref[r : r + 32, :]
                acc_w = acc_w + jnp.sum((w * w).reshape(4, 8, 128), axis=0)
                acc_u = acc_u + jnp.sum((u * u).reshape(4, 8, 128), axis=0)
        else:
            keep = (row == 0) & (lane >= l0) & (lane < l1)
            w = weight_ref[r0 : r0 + 8, :]
            u = update_ref[r0 : r0 + 8, :]
            acc_w = jnp.where(keep, w * w, 0.0)
            acc_u = jnp.where(keep, u * u, 0.0)
        vec = jnp.where((row == 0) & (lane == k), total(acc_w), vec)
        vec = jnp.where((row == 1) & (lane == k), total(acc_u), vec)
    pl.semaphore_wait(barrier, nt - 1 + nd - 1)
    recv_a[t] = vec
    copies = []
    for step in range(1, nt):
        copy = pltpu.make_async_remote_copy(
            src_ref=recv_a.at[t],
            dst_ref=recv_a.at[t],
            send_sem=send_a.at[step],
            recv_sem=got_a.at[t],
            device_id=(d, lax.rem(t + step, nt)),
            device_id_type=MESH,
        )
        copy.start()
        copies.append(copy)
    for step in range(1, nt):
        source = lax.rem(t + nt - step, nt)
        pltpu.make_async_remote_copy(
            src_ref=recv_a.at[source],
            dst_ref=recv_a.at[source],
            send_sem=send_a.at[step],
            recv_sem=got_a.at[source],
            device_id=(d, source),
            device_id_type=MESH,
        ).wait_recv()
    for copy in copies:
        copy.wait_send()
    acc = recv_a[0]
    for slot in range(1, nt):
        acc = acc + recv_a[slot]
    recv_b[d] = acc
    copies = []
    for step in range(1, nd):
        copy = pltpu.make_async_remote_copy(
            src_ref=recv_b.at[d],
            dst_ref=recv_b.at[d],
            send_sem=send_b.at[step],
            recv_sem=got_b.at[d],
            device_id=(lax.rem(d + step, nd), t),
            device_id_type=MESH,
        )
        copy.start()
        copies.append(copy)
    for step in range(1, nd):
        source = lax.rem(d + nd - step, nd)
        pltpu.make_async_remote_copy(
            src_ref=recv_b.at[source],
            dst_ref=recv_b.at[source],
            send_sem=send_b.at[step],
            recv_sem=got_b.at[source],
            device_id=(source, t),
            device_id_type=MESH,
        ).wait_recv()
    for copy in copies:
        copy.wait_send()
    acc = recv_b[0]
    for slot in range(1, nd):
        acc = acc + recv_b[slot]
    trust = jnp.sqrt(acc[0:1, :]) / jnp.sqrt(acc[1:2, :])
    trust = jnp.broadcast_to(trust, (8, 128))
    gain_scale = jnp.zeros((8, 128), jnp.float32)
    for k, (r0, r1, l0, l1) in enumerate(segments):
        factor = 0.1 * pick(trust, k)
        if l0 is None:
            for r in range(r0, r1, 32):
                w = weight_ref[r : r + 32, :]
                u = update_ref[r : r + 32, :]
                new = w - factor * u
                new_ref[r : r + 32, :] = new
                low_ref[r : r + 32, :] = new.astype(low_ref.dtype)
        else:
            gain_scale = jnp.where((lane >= l0) & (lane < l1), factor, gain_scale)
            tail = r0
    for r in range(tail, weight_ref.shape[0], 8):
        w = weight_ref[r : r + 8, :]
        u = update_ref[r : r + 8, :]
        scale = gain_scale if r == tail else jnp.zeros((8, 128), jnp.float32)
        new = w - scale * u
        new_ref[r : r + 8, :] = new
        low_ref[r : r + 8, :] = new.astype(low_ref.dtype)


def apply_step(weight_p, update, segments):
    nd = lax.axis_size("dp")
    nt = lax.axis_size("tensor")
    return pl.pallas_call(
        functools.partial(apply_kernel, nd, nt, segments),
        out_shape=(
            jax.ShapeDtypeStruct(weight_p.shape, jnp.float32),
            jax.ShapeDtypeStruct(weight_p.shape, jnp.bfloat16),
        ),
        in_specs=[pl.BlockSpec(memory_space=pltpu.VMEM)] * 2,
        out_specs=(
            pl.BlockSpec(memory_space=pltpu.VMEM),
            pl.BlockSpec(memory_space=pltpu.VMEM),
        ),
        scratch_shapes=[
            pltpu.VMEM((nt, 8, 128), jnp.float32),
            pltpu.VMEM((nd, 8, 128), jnp.float32),
            pltpu.SemaphoreType.DMA((nt,)),
            pltpu.SemaphoreType.DMA((nt,)),
            pltpu.SemaphoreType.DMA((nd,)),
            pltpu.SemaphoreType.DMA((nd,)),
        ],
        compiler_params=pltpu.CompilerParams(collective_id=0, has_side_effects=True),
    )(weight_p, update)


def on_device(*args):
    grads = args[:11]
    weights, first_moment, second_moment = args[11:]
    owners = lax.axis_size("dp")
    shapes = [g.shape[1:] for g in grads]
    pieces = [g.reshape(owners, -1) for g in grads]
    piece_len = [p.shape[1] for p in pieces]
    starts = [sum(piece_len[:k]) for k in range(11)]
    order = [k for k in range(11) if k not in GAIN_SEGMENTS] + list(GAIN_SEGMENTS)
    packed_len = sum(piece_len)
    padded = -(-packed_len // 1024) * 1024
    rows = padded // 128
    blocks = [(g.shape[1] // owners, g.shape[2]) if g.ndim == 3 else None for g in grads]

    def to_rows(x, a, b):
        lead = x.shape[0]
        if a % 8 == 0 and b % 128 == 0:
            x = x.reshape(lead, a // 8, 8, b // 128, 128).transpose(0, 1, 3, 2, 4)
            return x.reshape(lead, a * b // 128, 128)
        if b % 128 != 0 and a == 128:
            return x.transpose(0, 2, 1)
        return x.reshape(lead, a * b // 128, 128)

    def from_rows(y, a, b):
        lead = y.shape[0]
        if a % 8 == 0 and b % 128 == 0:
            y = y.reshape(lead, a // 8, b // 128, 8, 128).transpose(0, 1, 3, 2, 4)
            return y.reshape(lead, a, b)
        if b % 128 != 0 and a == 128:
            return y.transpose(0, 2, 1)
        return y.reshape(lead, a, b)

    big = [k for k in order if k not in GAIN_SEGMENTS]
    parts = [to_rows(grads[k][0].reshape((owners,) + blocks[k]), *blocks[k]) for k in big]
    gains = jnp.concatenate([pieces[k] for k in GAIN_SEGMENTS], axis=1)
    gain_width = gains.shape[1]
    parts.append(jnp.pad(gains, ((0, 0), (0, 128 - gain_width))).reshape(owners, 1, 128))
    used_rows = sum(p.shape[1] for p in parts)
    parts.append(jnp.zeros((owners, rows - used_rows, 128), gains.dtype))
    flat = jnp.concatenate(parts, axis=1)
    flat = with_layout_constraint(flat, Layout(major_to_minor=(0, 1, 2)))
    summed = lax.psum_scatter(flat, "dp", scatter_dimension=0, tiled=True)
    summed = lax.optimization_barrier(summed).reshape(-1)
    packed_start = {}
    offset = 0
    for k in order:
        packed_start[k] = offset
        offset += piece_len[k]
    segments = []
    for k in range(11):
        a, b = packed_start[k], packed_start[k] + piece_len[k]
        if a % 128 == 0 and b % 128 == 0:
            segments.append((a // 128, b // 128, None, None))
        else:
            segments.append((a // 128, a // 128 + 1, a % 128, (b - 1) % 128 + 1))

    def to_packed(row):
        out = []
        for k in big:
            seg = row[starts[k] : starts[k] + piece_len[k]].reshape((1,) + blocks[k])
            out.append(to_rows(seg, *blocks[k])[0])
        tail = [row[starts[k] : starts[k] + piece_len[k]] for k in GAIN_SEGMENTS]
        tail.append(jnp.zeros((128 - gain_width,), row.dtype))
        out.append(jnp.concatenate(tail).reshape(1, 128))
        out.append(jnp.zeros((rows - used_rows, 128), row.dtype))
        return jnp.concatenate(out, axis=0)

    def to_flat(block):
        out = []
        for k in range(11):
            r0, r1, l0, l1 = segments[k]
            if l0 is None:
                seg = from_rows(block[r0:r1].reshape(1, r1 - r0, 128), *blocks[k])
                out.append(seg.reshape(-1))
            else:
                out.append(block[r0, l0:l1])
        return jnp.concatenate(out).reshape(1, -1)

    grad = summed.reshape(rows, 128).astype(jnp.float32)
    weight_p = to_packed(weights.reshape(-1))
    first_p = to_packed(first_moment.reshape(-1))
    second_p = to_packed(second_moment.reshape(-1))
    new_first = 0.9 * first_p + 0.1 * grad
    new_second = 0.999 * second_p + 0.001 * grad * grad
    position = (
        lax.broadcasted_iota(jnp.int32, (rows, 128), 0) * 128
        + lax.broadcasted_iota(jnp.int32, (rows, 128), 1)
    )
    big_end = min(packed_start[k] for k in GAIN_SEGMENTS)
    update = new_first / (jnp.sqrt(new_second) + 1e-06)
    update = jnp.where(position < big_end, update + 0.01 * weight_p, update)
    new_weights, rounded = apply_step(weight_p, update, tuple(segments))
    gathered = lax.all_gather(rounded, "dp", axis=0, tiled=False)
    copies = [None] * 11
    for k in range(11):
        r0, r1, l0, l1 = segments[k]
        if l0 is None:
            part = from_rows(gathered[:, r0:r1, :], *blocks[k])
        else:
            part = gathered[:, r0, l0:l1]
        copies[k] = part.reshape(shapes[k])
    return (
        to_flat(new_weights),
        to_flat(new_first),
        to_flat(new_second),
        *copies,
    )


def solution(mesh):
    return jax.shard_map(
        on_device,
        mesh=mesh,
        in_specs=(
            P("dp", "tensor"),
            P("dp", None, "tensor"),
            P("dp", None, "tensor"),
            P("dp", None, "tensor"),
            P("dp", "tensor"),
            P("dp", None, "tensor"),
            P("dp", "tensor", None),
            P("dp", "tensor"),
            P("dp", None, "tensor"),
            P("dp", None, "tensor"),
            P("dp", "tensor", None),
            P("tensor", "dp"),
            P("tensor", "dp"),
            P("tensor", "dp"),
        ),
        out_specs=(
            P("tensor", "dp"),
            P("tensor", "dp"),
            P("tensor", "dp"),
            P("tensor"),
            P(None, "tensor"),
            P(None, "tensor"),
            P(None, "tensor"),
            P("tensor"),
            P(None, "tensor"),
            P("tensor", None),
            P("tensor"),
            P(None, "tensor"),
            P(None, "tensor"),
            P("tensor", None),
        ),
        check_vma=False,
    )
```

```python
import functools

import jax
import jax.numpy as jnp
from jax import lax
from jax.experimental import pallas as pl
from jax.experimental.pallas import tpu as pltpu
from jax.sharding import PartitionSpec as P

MESH = pl.DeviceIdType.MESH

GAIN_SEGMENTS = (0, 4, 7)


def apply_kernel(nd, nt, segments, weight_ref, update_ref, new_ref, low_ref, *scratch):
    recv_a, recv_b, send_a, got_a, send_b, got_b = scratch
    d = lax.axis_index("dp")
    t = lax.axis_index("tensor")
    barrier = pltpu.get_barrier_semaphore()
    for step in range(1, nt):
        pl.semaphore_signal(
            barrier, inc=1, device_id=(d, lax.rem(t + step, nt)), device_id_type=MESH
        )
    for step in range(1, nd):
        pl.semaphore_signal(
            barrier, inc=1, device_id=(lax.rem(d + step, nd), t), device_id_type=MESH
        )
    row = lax.broadcasted_iota(jnp.int32, (8, 128), 0)
    lane = lax.broadcasted_iota(jnp.int32, (8, 128), 1)

    def total(x):
        return jnp.sum(jnp.sum(x, axis=0, keepdims=True), axis=1, keepdims=True)

    def pick(vec, k):
        return total(jnp.where((row == 0) & (lane == k), vec, 0.0))

    vec = jnp.zeros((8, 128), jnp.float32)
    for k, (r0, r1, l0, l1) in enumerate(segments):
        if l0 is None:
            acc_w = jnp.zeros((8, 128), jnp.float32)
            acc_u = jnp.zeros((8, 128), jnp.float32)
            for r in range(r0, r1, 32):
                w = weight_ref[r : r + 32, :]
                u = update_ref[r : r + 32, :]
                acc_w = acc_w + jnp.sum((w * w).reshape(4, 8, 128), axis=0)
                acc_u = acc_u + jnp.sum((u * u).reshape(4, 8, 128), axis=0)
        else:
            keep = (row == 0) & (lane >= l0) & (lane < l1)
            w = weight_ref[r0 : r0 + 8, :]
            u = update_ref[r0 : r0 + 8, :]
            acc_w = jnp.where(keep, w * w, 0.0)
            acc_u = jnp.where(keep, u * u, 0.0)
        vec = jnp.where((row == 0) & (lane == k), total(acc_w), vec)
        vec = jnp.where((row == 1) & (lane == k), total(acc_u), vec)
    pl.semaphore_wait(barrier, nt - 1 + nd - 1)
    recv_a[t] = vec
    copies = []
    for step in range(1, nt):
        copy = pltpu.make_async_remote_copy(
            src_ref=recv_a.at[t],
            dst_ref=recv_a.at[t],
            send_sem=send_a.at[step],
            recv_sem=got_a.at[t],
            device_id=(d, lax.rem(t + step, nt)),
            device_id_type=MESH,
        )
        copy.start()
        copies.append(copy)
    for step in range(1, nt):
        source = lax.rem(t + nt - step, nt)
        pltpu.make_async_remote_copy(
            src_ref=recv_a.at[source],
            dst_ref=recv_a.at[source],
            send_sem=send_a.at[step],
            recv_sem=got_a.at[source],
            device_id=(d, source),
            device_id_type=MESH,
        ).wait_recv()
    for copy in copies:
        copy.wait_send()
    acc = recv_a[0]
    for slot in range(1, nt):
        acc = acc + recv_a[slot]
    recv_b[d] = acc
    copies = []
    for step in range(1, nd):
        copy = pltpu.make_async_remote_copy(
            src_ref=recv_b.at[d],
            dst_ref=recv_b.at[d],
            send_sem=send_b.at[step],
            recv_sem=got_b.at[d],
            device_id=(lax.rem(d + step, nd), t),
            device_id_type=MESH,
        )
        copy.start()
        copies.append(copy)
    for step in range(1, nd):
        source = lax.rem(d + nd - step, nd)
        pltpu.make_async_remote_copy(
            src_ref=recv_b.at[source],
            dst_ref=recv_b.at[source],
            send_sem=send_b.at[step],
            recv_sem=got_b.at[source],
            device_id=(source, t),
            device_id_type=MESH,
        ).wait_recv()
    for copy in copies:
        copy.wait_send()
    acc = recv_b[0]
    for slot in range(1, nd):
        acc = acc + recv_b[slot]
    trust = jnp.sqrt(acc[0:1, :]) / jnp.sqrt(acc[1:2, :])
    trust = jnp.broadcast_to(trust, (8, 128))
    gain_scale = jnp.zeros((8, 128), jnp.float32)
    for k, (r0, r1, l0, l1) in enumerate(segments):
        factor = 0.1 * pick(trust, k)
        if l0 is None:
            for r in range(r0, r1, 32):
                w = weight_ref[r : r + 32, :]
                u = update_ref[r : r + 32, :]
                new = w - factor * u
                new_ref[r : r + 32, :] = new
                low_ref[r : r + 32, :] = new.astype(low_ref.dtype)
        else:
            gain_scale = jnp.where((lane >= l0) & (lane < l1), factor, gain_scale)
            tail = r0
    for r in range(tail, weight_ref.shape[0], 8):
        w = weight_ref[r : r + 8, :]
        u = update_ref[r : r + 8, :]
        scale = gain_scale if r == tail else jnp.zeros((8, 128), jnp.float32)
        new = w - scale * u
        new_ref[r : r + 8, :] = new
        low_ref[r : r + 8, :] = new.astype(low_ref.dtype)


def pack_kernel(plan, *refs):
    out_ref = refs[-1]
    owners = out_ref.shape[0]

    def body(j, carry):
        for index, (r0, a, b, raw) in enumerate(plan):
            src = refs[index]
            if raw:
                start = pl.multiple_of(j * a, a)
                for ct in range(b // 128):
                    out_ref[j, r0 + ct * a : r0 + (ct + 1) * a, :] = src[
                        0, pl.ds(start, a), ct * 128 : (ct + 1) * 128
                    ]
            else:
                out_ref[j, r0 : r0 + a, :] = src[j]
        return carry

    lax.fori_loop(0, owners, body, 0)


def pack_rows(inputs, plan, owners, rows):
    return pl.pallas_call(
        functools.partial(pack_kernel, plan),
        out_shape=jax.ShapeDtypeStruct((owners, rows, 128), jnp.bfloat16),
        in_specs=[pl.BlockSpec(memory_space=pltpu.VMEM)] * len(inputs),
        out_specs=pl.BlockSpec(memory_space=pltpu.VMEM),
    )(*inputs)


def apply_step(weight_p, update, segments):
    nd = lax.axis_size("dp")
    nt = lax.axis_size("tensor")
    return pl.pallas_call(
        functools.partial(apply_kernel, nd, nt, segments),
        out_shape=(
            jax.ShapeDtypeStruct(weight_p.shape, jnp.float32),
            jax.ShapeDtypeStruct(weight_p.shape, jnp.bfloat16),
        ),
        in_specs=[pl.BlockSpec(memory_space=pltpu.VMEM)] * 2,
        out_specs=(
            pl.BlockSpec(memory_space=pltpu.VMEM),
            pl.BlockSpec(memory_space=pltpu.VMEM),
        ),
        scratch_shapes=[
            pltpu.VMEM((nt, 8, 128), jnp.float32),
            pltpu.VMEM((nd, 8, 128), jnp.float32),
            pltpu.SemaphoreType.DMA((nt,)),
            pltpu.SemaphoreType.DMA((nt,)),
            pltpu.SemaphoreType.DMA((nd,)),
            pltpu.SemaphoreType.DMA((nd,)),
        ],
        compiler_params=pltpu.CompilerParams(collective_id=0, has_side_effects=True),
    )(weight_p, update)


def on_device(*args):
    grads = args[:11]
    weights, first_moment, second_moment = args[11:]
    owners = lax.axis_size("dp")
    shapes = [g.shape[1:] for g in grads]
    pieces = [g.reshape(owners, -1) for g in grads]
    piece_len = [p.shape[1] for p in pieces]
    starts = [sum(piece_len[:k]) for k in range(11)]
    order = [k for k in range(11) if k not in GAIN_SEGMENTS] + list(GAIN_SEGMENTS)
    packed_len = sum(piece_len)
    padded = -(-packed_len // 1024) * 1024
    rows = padded // 128
    blocks = [(g.shape[1] // owners, g.shape[2]) if g.ndim == 3 else None for g in grads]

    def to_rows(x, a, b):
        lead = x.shape[0]
        if a % 8 == 0 and b % 128 == 0:
            x = x.reshape(lead, a, b // 128, 128).transpose(0, 2, 1, 3)
            return x.reshape(lead, a * b // 128, 128)
        if b % 128 != 0 and a == 128:
            return x.transpose(0, 2, 1)
        return x.reshape(lead, a * b // 128, 128)

    def from_rows(y, a, b):
        lead = y.shape[0]
        if a % 8 == 0 and b % 128 == 0:
            y = y.reshape(lead, b // 128, a, 128).transpose(0, 2, 1, 3)
            return y.reshape(lead, a, b)
        if b % 128 != 0 and a == 128:
            return y.transpose(0, 2, 1)
        return y.reshape(lead, a, b)

    big = [k for k in order if k not in GAIN_SEGMENTS]
    inputs = []
    plan = []
    row = 0
    for k in big:
        a, b = blocks[k]
        if a % 16 == 0 and b % 128 == 0:
            inputs.append(grads[k])
            plan.append((row, a, b, True))
        else:
            inputs.append(to_rows(grads[k][0].reshape((owners,) + blocks[k]), a, b))
            plan.append((row, a * b // 128, 128, False))
        row += a * b // 128
    gains = jnp.concatenate([pieces[k] for k in GAIN_SEGMENTS], axis=1)
    gain_width = gains.shape[1]
    used_rows = row + 1
    tail = jnp.pad(gains, ((0, 0), (0, 128 - gain_width))).reshape(owners, 1, 128)
    tail = jnp.pad(tail, ((0, 0), (0, rows - used_rows), (0, 0)))
    inputs.append(tail)
    plan.append((row, rows - row, 128, False))
    flat = pack_rows(inputs, tuple(plan), owners, rows)
    summed = lax.psum_scatter(flat, "dp", scatter_dimension=0, tiled=True)
    summed = lax.optimization_barrier(summed).reshape(-1)
    packed_start = {}
    offset = 0
    for k in order:
        packed_start[k] = offset
        offset += piece_len[k]
    segments = []
    for k in range(11):
        a, b = packed_start[k], packed_start[k] + piece_len[k]
        if a % 128 == 0 and b % 128 == 0:
            segments.append((a // 128, b // 128, None, None))
        else:
            segments.append((a // 128, a // 128 + 1, a % 128, (b - 1) % 128 + 1))

    def to_packed(row):
        out = []
        for k in big:
            seg = row[starts[k] : starts[k] + piece_len[k]].reshape((1,) + blocks[k])
            out.append(to_rows(seg, *blocks[k])[0])
        tail = [row[starts[k] : starts[k] + piece_len[k]] for k in GAIN_SEGMENTS]
        tail.append(jnp.zeros((128 - gain_width,), row.dtype))
        out.append(jnp.concatenate(tail).reshape(1, 128))
        out.append(jnp.zeros((rows - used_rows, 128), row.dtype))
        return jnp.concatenate(out, axis=0)

    def to_flat(block):
        out = []
        for k in range(11):
            r0, r1, l0, l1 = segments[k]
            if l0 is None:
                seg = from_rows(block[r0:r1].reshape(1, r1 - r0, 128), *blocks[k])
                out.append(seg.reshape(-1))
            else:
                out.append(block[r0, l0:l1])
        return jnp.concatenate(out).reshape(1, -1)

    grad = summed.reshape(rows, 128).astype(jnp.float32)
    weight_p = to_packed(weights.reshape(-1))
    first_p = to_packed(first_moment.reshape(-1))
    second_p = to_packed(second_moment.reshape(-1))
    new_first = 0.9 * first_p + 0.1 * grad
    new_second = 0.999 * second_p + 0.001 * grad * grad
    position = (
        lax.broadcasted_iota(jnp.int32, (rows, 128), 0) * 128
        + lax.broadcasted_iota(jnp.int32, (rows, 128), 1)
    )
    big_end = min(packed_start[k] for k in GAIN_SEGMENTS)
    update = new_first / (jnp.sqrt(new_second) + 1e-06)
    update = jnp.where(position < big_end, update + 0.01 * weight_p, update)
    new_weights, rounded = apply_step(weight_p, update, tuple(segments))
    gathered = lax.all_gather(rounded, "dp", axis=0, tiled=False)
    copies = [None] * 11
    for k in range(11):
        r0, r1, l0, l1 = segments[k]
        if l0 is None:
            part = from_rows(gathered[:, r0:r1, :], *blocks[k])
        else:
            part = gathered[:, r0, l0:l1]
        copies[k] = part.reshape(shapes[k])
    return (
        to_flat(new_weights),
        to_flat(new_first),
        to_flat(new_second),
        *copies,
    )


def solution(mesh):
    return jax.shard_map(
        on_device,
        mesh=mesh,
        in_specs=(
            P("dp", "tensor"),
            P("dp", None, "tensor"),
            P("dp", None, "tensor"),
            P("dp", None, "tensor"),
            P("dp", "tensor"),
            P("dp", None, "tensor"),
            P("dp", "tensor", None),
            P("dp", "tensor"),
            P("dp", None, "tensor"),
            P("dp", None, "tensor"),
            P("dp", "tensor", None),
            P("tensor", "dp"),
            P("tensor", "dp"),
            P("tensor", "dp"),
        ),
        out_specs=(
            P("tensor", "dp"),
            P("tensor", "dp"),
            P("tensor", "dp"),
            P("tensor"),
            P(None, "tensor"),
            P(None, "tensor"),
            P(None, "tensor"),
            P("tensor"),
            P(None, "tensor"),
            P("tensor", None),
            P("tensor"),
            P(None, "tensor"),
            P(None, "tensor"),
            P("tensor", None),
        ),
        check_vma=False,
    )
```

```python
import functools

import jax
import jax.numpy as jnp
from jax import lax
from jax.experimental import pallas as pl
from jax.experimental.pallas import tpu as pltpu
from jax.sharding import PartitionSpec as P

MESH = pl.DeviceIdType.MESH

GAIN_SEGMENTS = (0, 4, 7)


def apply_kernel(nd, nt, segments, weight_ref, update_ref, new_ref, low_ref, *scratch):
    recv_a, recv_b, send_a, got_a, send_b, got_b = scratch
    d = lax.axis_index("dp")
    t = lax.axis_index("tensor")
    barrier = pltpu.get_barrier_semaphore()
    for step in range(1, nt):
        pl.semaphore_signal(
            barrier, inc=1, device_id=(d, lax.rem(t + step, nt)), device_id_type=MESH
        )
    for step in range(1, nd):
        pl.semaphore_signal(
            barrier, inc=1, device_id=(lax.rem(d + step, nd), t), device_id_type=MESH
        )
    row = lax.broadcasted_iota(jnp.int32, (8, 128), 0)
    lane = lax.broadcasted_iota(jnp.int32, (8, 128), 1)

    def total(x):
        return jnp.sum(jnp.sum(x, axis=0, keepdims=True), axis=1, keepdims=True)

    def pick(vec, k):
        return total(jnp.where((row == 0) & (lane == k), vec, 0.0))

    vec = jnp.zeros((8, 128), jnp.float32)
    for k, (r0, r1, l0, l1) in enumerate(segments):
        if l0 is None:
            acc_w = jnp.zeros((8, 128), jnp.float32)
            acc_u = jnp.zeros((8, 128), jnp.float32)
            for r in range(r0, r1, 32):
                w = weight_ref[r : r + 32, :]
                u = update_ref[r : r + 32, :]
                acc_w = acc_w + jnp.sum((w * w).reshape(4, 8, 128), axis=0)
                acc_u = acc_u + jnp.sum((u * u).reshape(4, 8, 128), axis=0)
        else:
            keep = (row == 0) & (lane >= l0) & (lane < l1)
            w = weight_ref[r0 : r0 + 8, :]
            u = update_ref[r0 : r0 + 8, :]
            acc_w = jnp.where(keep, w * w, 0.0)
            acc_u = jnp.where(keep, u * u, 0.0)
        vec = jnp.where((row == 0) & (lane == k), total(acc_w), vec)
        vec = jnp.where((row == 1) & (lane == k), total(acc_u), vec)
    pl.semaphore_wait(barrier, nt - 1 + nd - 1)
    recv_a[t] = vec
    copies = []
    for step in range(1, nt):
        copy = pltpu.make_async_remote_copy(
            src_ref=recv_a.at[t],
            dst_ref=recv_a.at[t],
            send_sem=send_a.at[step],
            recv_sem=got_a.at[t],
            device_id=(d, lax.rem(t + step, nt)),
            device_id_type=MESH,
        )
        copy.start()
        copies.append(copy)
    for step in range(1, nt):
        source = lax.rem(t + nt - step, nt)
        pltpu.make_async_remote_copy(
            src_ref=recv_a.at[source],
            dst_ref=recv_a.at[source],
            send_sem=send_a.at[step],
            recv_sem=got_a.at[source],
            device_id=(d, source),
            device_id_type=MESH,
        ).wait_recv()
    for copy in copies:
        copy.wait_send()
    acc = recv_a[0]
    for slot in range(1, nt):
        acc = acc + recv_a[slot]
    recv_b[d] = acc
    copies = []
    for step in range(1, nd):
        copy = pltpu.make_async_remote_copy(
            src_ref=recv_b.at[d],
            dst_ref=recv_b.at[d],
            send_sem=send_b.at[step],
            recv_sem=got_b.at[d],
            device_id=(lax.rem(d + step, nd), t),
            device_id_type=MESH,
        )
        copy.start()
        copies.append(copy)
    for step in range(1, nd):
        source = lax.rem(d + nd - step, nd)
        pltpu.make_async_remote_copy(
            src_ref=recv_b.at[source],
            dst_ref=recv_b.at[source],
            send_sem=send_b.at[step],
            recv_sem=got_b.at[source],
            device_id=(source, t),
            device_id_type=MESH,
        ).wait_recv()
    for copy in copies:
        copy.wait_send()
    acc = recv_b[0]
    for slot in range(1, nd):
        acc = acc + recv_b[slot]
    trust = jnp.sqrt(acc[0:1, :]) / jnp.sqrt(acc[1:2, :])
    trust = jnp.broadcast_to(trust, (8, 128))
    gain_scale = jnp.zeros((8, 128), jnp.float32)
    for k, (r0, r1, l0, l1) in enumerate(segments):
        factor = 0.1 * pick(trust, k)
        if l0 is None:
            for r in range(r0, r1, 32):
                w = weight_ref[r : r + 32, :]
                u = update_ref[r : r + 32, :]
                new = w - factor * u
                new_ref[r : r + 32, :] = new
                low_ref[r : r + 32, :] = new.astype(low_ref.dtype)
        else:
            gain_scale = jnp.where((lane >= l0) & (lane < l1), factor, gain_scale)
            tail = r0
    for r in range(tail, weight_ref.shape[0], 8):
        w = weight_ref[r : r + 8, :]
        u = update_ref[r : r + 8, :]
        scale = gain_scale if r == tail else jnp.zeros((8, 128), jnp.float32)
        new = w - scale * u
        new_ref[r : r + 8, :] = new
        low_ref[r : r + 8, :] = new.astype(low_ref.dtype)


def pack_kernel(plan, *refs):
    out_ref = refs[-1]
    owners = out_ref.shape[0]

    def body(j, carry):
        for index, (r0, a, b, raw) in enumerate(plan):
            src = refs[index]
            if raw:
                start = pl.multiple_of(j * a, a)
                for rt in range(a // 8):
                    for ct in range(b // 128):
                        at = r0 + (rt * (b // 128) + ct) * 8
                        out_ref[j, at : at + 8, :] = src[
                            0, pl.ds(start + rt * 8, 8), ct * 128 : (ct + 1) * 128
                        ]
            else:
                out_ref[j, r0 : r0 + a, :] = src[j]
        return carry

    lax.fori_loop(0, owners, body, 0)


def pack_rows(inputs, plan, owners, rows):
    return pl.pallas_call(
        functools.partial(pack_kernel, plan),
        out_shape=jax.ShapeDtypeStruct((owners, rows, 128), jnp.bfloat16),
        in_specs=[pl.BlockSpec(memory_space=pltpu.VMEM)] * len(inputs),
        out_specs=pl.BlockSpec(memory_space=pltpu.VMEM),
    )(*inputs)


def apply_step(weight_p, update, segments):
    nd = lax.axis_size("dp")
    nt = lax.axis_size("tensor")
    return pl.pallas_call(
        functools.partial(apply_kernel, nd, nt, segments),
        out_shape=(
            jax.ShapeDtypeStruct(weight_p.shape, jnp.float32),
            jax.ShapeDtypeStruct(weight_p.shape, jnp.bfloat16),
        ),
        in_specs=[pl.BlockSpec(memory_space=pltpu.VMEM)] * 2,
        out_specs=(
            pl.BlockSpec(memory_space=pltpu.VMEM),
            pl.BlockSpec(memory_space=pltpu.VMEM),
        ),
        scratch_shapes=[
            pltpu.VMEM((nt, 8, 128), jnp.float32),
            pltpu.VMEM((nd, 8, 128), jnp.float32),
            pltpu.SemaphoreType.DMA((nt,)),
            pltpu.SemaphoreType.DMA((nt,)),
            pltpu.SemaphoreType.DMA((nd,)),
            pltpu.SemaphoreType.DMA((nd,)),
        ],
        compiler_params=pltpu.CompilerParams(collective_id=0, has_side_effects=True),
    )(weight_p, update)


def on_device(*args):
    grads = args[:11]
    weights, first_moment, second_moment = args[11:]
    owners = lax.axis_size("dp")
    shapes = [g.shape[1:] for g in grads]
    pieces = [g.reshape(owners, -1) for g in grads]
    piece_len = [p.shape[1] for p in pieces]
    starts = [sum(piece_len[:k]) for k in range(11)]
    order = [k for k in range(11) if k not in GAIN_SEGMENTS] + list(GAIN_SEGMENTS)
    packed_len = sum(piece_len)
    padded = -(-packed_len // 1024) * 1024
    rows = padded // 128
    blocks = [(g.shape[1] // owners, g.shape[2]) if g.ndim == 3 else None for g in grads]

    def to_rows(x, a, b):
        lead = x.shape[0]
        if a % 8 == 0 and b % 128 == 0:
            x = x.reshape(lead, a // 8, 8, b // 128, 128).transpose(0, 1, 3, 2, 4)
            return x.reshape(lead, a * b // 128, 128)
        if b % 128 != 0 and a == 128:
            return x.transpose(0, 2, 1)
        return x.reshape(lead, a * b // 128, 128)

    def from_rows(y, a, b):
        lead = y.shape[0]
        if a % 8 == 0 and b % 128 == 0:
            y = y.reshape(lead, a // 8, b // 128, 8, 128).transpose(0, 1, 3, 2, 4)
            return y.reshape(lead, a, b)
        if b % 128 != 0 and a == 128:
            return y.transpose(0, 2, 1)
        return y.reshape(lead, a, b)

    big = [k for k in order if k not in GAIN_SEGMENTS]
    inputs = []
    plan = []
    row = 0
    for k in big:
        a, b = blocks[k]
        if a % 16 == 0 and b % 128 == 0:
            inputs.append(grads[k])
            plan.append((row, a, b, True))
        else:
            inputs.append(to_rows(grads[k][0].reshape((owners,) + blocks[k]), a, b))
            plan.append((row, a * b // 128, 128, False))
        row += a * b // 128
    gains = jnp.concatenate([pieces[k] for k in GAIN_SEGMENTS], axis=1)
    gain_width = gains.shape[1]
    used_rows = row + 1
    tail = jnp.pad(gains, ((0, 0), (0, 128 - gain_width))).reshape(owners, 1, 128)
    tail = jnp.pad(tail, ((0, 0), (0, rows - used_rows), (0, 0)))
    inputs.append(tail)
    plan.append((row, rows - row, 128, False))
    flat = pack_rows(inputs, tuple(plan), owners, rows)
    summed = lax.psum_scatter(flat, "dp", scatter_dimension=0, tiled=True)
    summed = lax.optimization_barrier(summed).reshape(-1)
    packed_start = {}
    offset = 0
    for k in order:
        packed_start[k] = offset
        offset += piece_len[k]
    segments = []
    for k in range(11):
        a, b = packed_start[k], packed_start[k] + piece_len[k]
        if a % 128 == 0 and b % 128 == 0:
            segments.append((a // 128, b // 128, None, None))
        else:
            segments.append((a // 128, a // 128 + 1, a % 128, (b - 1) % 128 + 1))

    def to_packed(row):
        out = []
        for k in big:
            seg = row[starts[k] : starts[k] + piece_len[k]].reshape((1,) + blocks[k])
            out.append(to_rows(seg, *blocks[k])[0])
        tail = [row[starts[k] : starts[k] + piece_len[k]] for k in GAIN_SEGMENTS]
        tail.append(jnp.zeros((128 - gain_width,), row.dtype))
        out.append(jnp.concatenate(tail).reshape(1, 128))
        out.append(jnp.zeros((rows - used_rows, 128), row.dtype))
        return jnp.concatenate(out, axis=0)

    def to_flat(block):
        out = []
        for k in range(11):
            r0, r1, l0, l1 = segments[k]
            if l0 is None:
                seg = from_rows(block[r0:r1].reshape(1, r1 - r0, 128), *blocks[k])
                out.append(seg.reshape(-1))
            else:
                out.append(block[r0, l0:l1])
        return jnp.concatenate(out).reshape(1, -1)

    grad = summed.reshape(rows, 128).astype(jnp.float32)
    weight_p = to_packed(weights.reshape(-1))
    first_p = to_packed(first_moment.reshape(-1))
    second_p = to_packed(second_moment.reshape(-1))
    new_first = 0.9 * first_p + 0.1 * grad
    new_second = 0.999 * second_p + 0.001 * grad * grad
    position = (
        lax.broadcasted_iota(jnp.int32, (rows, 128), 0) * 128
        + lax.broadcasted_iota(jnp.int32, (rows, 128), 1)
    )
    big_end = min(packed_start[k] for k in GAIN_SEGMENTS)
    update = new_first / (jnp.sqrt(new_second) + 1e-06)
    update = jnp.where(position < big_end, update + 0.01 * weight_p, update)
    new_weights, rounded = apply_step(weight_p, update, tuple(segments))
    gathered = lax.all_gather(rounded, "dp", axis=0, tiled=False)
    copies = [None] * 11
    for k in range(11):
        r0, r1, l0, l1 = segments[k]
        if l0 is None:
            part = from_rows(gathered[:, r0:r1, :], *blocks[k])
        else:
            part = gathered[:, r0, l0:l1]
        copies[k] = part.reshape(shapes[k])
    return (
        to_flat(new_weights),
        to_flat(new_first),
        to_flat(new_second),
        *copies,
    )


def solution(mesh):
    return jax.shard_map(
        on_device,
        mesh=mesh,
        in_specs=(
            P("dp", "tensor"),
            P("dp", None, "tensor"),
            P("dp", None, "tensor"),
            P("dp", None, "tensor"),
            P("dp", "tensor"),
            P("dp", None, "tensor"),
            P("dp", "tensor", None),
            P("dp", "tensor"),
            P("dp", None, "tensor"),
            P("dp", None, "tensor"),
            P("dp", "tensor", None),
            P("tensor", "dp"),
            P("tensor", "dp"),
            P("tensor", "dp"),
        ),
        out_specs=(
            P("tensor", "dp"),
            P("tensor", "dp"),
            P("tensor", "dp"),
            P("tensor"),
            P(None, "tensor"),
            P(None, "tensor"),
            P(None, "tensor"),
            P("tensor"),
            P(None, "tensor"),
            P("tensor", None),
            P("tensor"),
            P(None, "tensor"),
            P(None, "tensor"),
            P("tensor", None),
        ),
        check_vma=False,
    )
```

```python
import functools

import jax
import jax.numpy as jnp
from jax import lax
from jax.experimental import pallas as pl
from jax.experimental.pallas import tpu as pltpu
from jax.sharding import PartitionSpec as P

MESH = pl.DeviceIdType.MESH

GAIN_SEGMENTS = (0, 4, 7)


def apply_kernel(nd, nt, segments, weight_ref, update_ref, new_ref, low_ref, *scratch):
    recv_a, recv_b, send_a, got_a, send_b, got_b = scratch
    d = lax.axis_index("dp")
    t = lax.axis_index("tensor")
    barrier = pltpu.get_barrier_semaphore()
    for step in range(1, nt):
        pl.semaphore_signal(
            barrier, inc=1, device_id=(d, lax.rem(t + step, nt)), device_id_type=MESH
        )
    for step in range(1, nd):
        pl.semaphore_signal(
            barrier, inc=1, device_id=(lax.rem(d + step, nd), t), device_id_type=MESH
        )
    row = lax.broadcasted_iota(jnp.int32, (8, 128), 0)
    lane = lax.broadcasted_iota(jnp.int32, (8, 128), 1)

    def total(x):
        return jnp.sum(jnp.sum(x, axis=0, keepdims=True), axis=1, keepdims=True)

    def pick(vec, k):
        return total(jnp.where((row == 0) & (lane == k), vec, 0.0))

    vec = jnp.zeros((8, 128), jnp.float32)
    for k, (r0, r1, l0, l1) in enumerate(segments):
        if l0 is None:
            acc_w = jnp.zeros((8, 128), jnp.float32)
            acc_u = jnp.zeros((8, 128), jnp.float32)
            for r in range(r0, r1, 32):
                w = weight_ref[r : r + 32, :]
                u = update_ref[r : r + 32, :]
                acc_w = acc_w + jnp.sum((w * w).reshape(4, 8, 128), axis=0)
                acc_u = acc_u + jnp.sum((u * u).reshape(4, 8, 128), axis=0)
        else:
            keep = (row == 0) & (lane >= l0) & (lane < l1)
            w = weight_ref[r0 : r0 + 8, :]
            u = update_ref[r0 : r0 + 8, :]
            acc_w = jnp.where(keep, w * w, 0.0)
            acc_u = jnp.where(keep, u * u, 0.0)
        vec = jnp.where((row == 0) & (lane == k), total(acc_w), vec)
        vec = jnp.where((row == 1) & (lane == k), total(acc_u), vec)
    pl.semaphore_wait(barrier, nt - 1 + nd - 1)
    recv_a[t] = vec
    copies = []
    for step in range(1, nt):
        copy = pltpu.make_async_remote_copy(
            src_ref=recv_a.at[t],
            dst_ref=recv_a.at[t],
            send_sem=send_a.at[step],
            recv_sem=got_a.at[t],
            device_id=(d, lax.rem(t + step, nt)),
            device_id_type=MESH,
        )
        copy.start()
        copies.append(copy)
    for step in range(1, nt):
        source = lax.rem(t + nt - step, nt)
        pltpu.make_async_remote_copy(
            src_ref=recv_a.at[source],
            dst_ref=recv_a.at[source],
            send_sem=send_a.at[step],
            recv_sem=got_a.at[source],
            device_id=(d, source),
            device_id_type=MESH,
        ).wait_recv()
    for copy in copies:
        copy.wait_send()
    acc = recv_a[0]
    for slot in range(1, nt):
        acc = acc + recv_a[slot]
    recv_b[d] = acc
    copies = []
    for step in range(1, nd):
        copy = pltpu.make_async_remote_copy(
            src_ref=recv_b.at[d],
            dst_ref=recv_b.at[d],
            send_sem=send_b.at[step],
            recv_sem=got_b.at[d],
            device_id=(lax.rem(d + step, nd), t),
            device_id_type=MESH,
        )
        copy.start()
        copies.append(copy)
    for step in range(1, nd):
        source = lax.rem(d + nd - step, nd)
        pltpu.make_async_remote_copy(
            src_ref=recv_b.at[source],
            dst_ref=recv_b.at[source],
            send_sem=send_b.at[step],
            recv_sem=got_b.at[source],
            device_id=(source, t),
            device_id_type=MESH,
        ).wait_recv()
    for copy in copies:
        copy.wait_send()
    acc = recv_b[0]
    for slot in range(1, nd):
        acc = acc + recv_b[slot]
    trust = jnp.sqrt(acc[0:1, :]) / jnp.sqrt(acc[1:2, :])
    trust = jnp.broadcast_to(trust, (8, 128))
    gain_scale = jnp.zeros((8, 128), jnp.float32)
    for k, (r0, r1, l0, l1) in enumerate(segments):
        factor = 0.1 * pick(trust, k)
        if l0 is None:
            for r in range(r0, r1, 32):
                w = weight_ref[r : r + 32, :]
                u = update_ref[r : r + 32, :]
                new = w - factor * u
                new_ref[r : r + 32, :] = new
                low_ref[r : r + 32, :] = new.astype(low_ref.dtype)
        else:
            gain_scale = jnp.where((lane >= l0) & (lane < l1), factor, gain_scale)
            tail = r0
    for r in range(tail, weight_ref.shape[0], 8):
        w = weight_ref[r : r + 8, :]
        u = update_ref[r : r + 8, :]
        scale = gain_scale if r == tail else jnp.zeros((8, 128), jnp.float32)
        new = w - scale * u
        new_ref[r : r + 8, :] = new
        low_ref[r : r + 8, :] = new.astype(low_ref.dtype)


def pack_kernel(plan, *refs):
    out_ref = refs[-1]
    owners = out_ref.shape[0]

    def body(j, carry):
        for index, (r0, a, b, raw) in enumerate(plan):
            src = refs[index]
            if raw:
                start = pl.multiple_of(j * a, a)
                for rt in range(a // 8):
                    for ct in range(b // 128):
                        at = r0 + (rt * (b // 128) + ct) * 8
                        out_ref[j, at : at + 8, :] = src[
                            0, pl.ds(start + rt * 8, 8), ct * 128 : (ct + 1) * 128
                        ]
            else:
                out_ref[j, r0 : r0 + a, :] = src[j]
        return carry

    lax.fori_loop(0, owners, body, 0)


def pack_rows(inputs, plan, owners, rows):
    return pl.pallas_call(
        functools.partial(pack_kernel, plan),
        out_shape=jax.ShapeDtypeStruct((owners, rows, 128), jnp.bfloat16),
        in_specs=[pl.BlockSpec(memory_space=pltpu.VMEM)] * len(inputs),
        out_specs=pl.BlockSpec(memory_space=pltpu.VMEM),
    )(*inputs)


def apply_step(weight_p, update, segments):
    nd = lax.axis_size("dp")
    nt = lax.axis_size("tensor")
    return pl.pallas_call(
        functools.partial(apply_kernel, nd, nt, segments),
        out_shape=(
            jax.ShapeDtypeStruct(weight_p.shape, jnp.float32),
            jax.ShapeDtypeStruct(weight_p.shape, jnp.bfloat16),
        ),
        in_specs=[pl.BlockSpec(memory_space=pltpu.VMEM)] * 2,
        out_specs=(
            pl.BlockSpec(memory_space=pltpu.VMEM),
            pl.BlockSpec(memory_space=pltpu.VMEM),
        ),
        scratch_shapes=[
            pltpu.VMEM((nt, 8, 128), jnp.float32),
            pltpu.VMEM((nd, 8, 128), jnp.float32),
            pltpu.SemaphoreType.DMA((nt,)),
            pltpu.SemaphoreType.DMA((nt,)),
            pltpu.SemaphoreType.DMA((nd,)),
            pltpu.SemaphoreType.DMA((nd,)),
        ],
        compiler_params=pltpu.CompilerParams(collective_id=0, has_side_effects=True),
    )(weight_p, update)


def on_device(*args):
    grads = args[:11]
    weights, first_moment, second_moment = args[11:]
    owners = lax.axis_size("dp")
    shapes = [g.shape[1:] for g in grads]
    pieces = [g.reshape(owners, -1) for g in grads]
    piece_len = [p.shape[1] for p in pieces]
    starts = [sum(piece_len[:k]) for k in range(11)]
    order = [k for k in range(11) if k not in GAIN_SEGMENTS] + list(GAIN_SEGMENTS)
    packed_len = sum(piece_len)
    padded = -(-packed_len // 1024) * 1024
    rows = padded // 128
    blocks = [(g.shape[1] // owners, g.shape[2]) if g.ndim == 3 else None for g in grads]

    def to_rows(x, a, b):
        lead = x.shape[0]
        if a % 8 == 0 and b % 128 == 0:
            x = x.reshape(lead, a // 8, 8, b // 128, 128).transpose(0, 1, 3, 2, 4)
            return x.reshape(lead, a * b // 128, 128)
        if b % 128 != 0 and a == 128:
            return x.transpose(0, 2, 1)
        return x.reshape(lead, a * b // 128, 128)

    def from_rows(y, a, b):
        lead = y.shape[0]
        if a % 8 == 0 and b % 128 == 0:
            y = y.reshape(lead, a // 8, b // 128, 8, 128).transpose(0, 1, 3, 2, 4)
            return y.reshape(lead, a, b)
        if b % 128 != 0 and a == 128:
            return y.transpose(0, 2, 1)
        return y.reshape(lead, a, b)

    big = [k for k in order if k not in GAIN_SEGMENTS]
    inputs = []
    plan = []
    row = 0
    for k in big:
        a, b = blocks[k]
        if a % 16 == 0 and b % 128 == 0:
            inputs.append(grads[k])
            plan.append((row, a, b, True))
        else:
            inputs.append(to_rows(grads[k][0].reshape((owners,) + blocks[k]), a, b))
            plan.append((row, a * b // 128, 128, False))
        row += a * b // 128
    gains = jnp.concatenate([pieces[k] for k in GAIN_SEGMENTS], axis=1)
    gain_width = gains.shape[1]
    used_rows = row + 1
    tail = jnp.pad(gains, ((0, 0), (0, 128 - gain_width))).reshape(owners, 1, 128)
    tail = jnp.pad(tail, ((0, 0), (0, rows - used_rows), (0, 0)))
    inputs.append(tail)
    plan.append((row, rows - row, 128, False))
    flat = pack_rows(inputs, tuple(plan), owners, rows)
    summed = lax.psum_scatter(flat, "dp", scatter_dimension=0, tiled=True)
    summed = lax.optimization_barrier(summed).reshape(-1)
    packed_start = {}
    offset = 0
    for k in order:
        packed_start[k] = offset
        offset += piece_len[k]
    segments = []
    for k in range(11):
        a, b = packed_start[k], packed_start[k] + piece_len[k]
        if a % 128 == 0 and b % 128 == 0:
            segments.append((a // 128, b // 128, None, None))
        else:
            segments.append((a // 128, a // 128 + 1, a % 128, (b - 1) % 128 + 1))

    def to_packed(row):
        out = []
        for k in big:
            seg = row[starts[k] : starts[k] + piece_len[k]].reshape((1,) + blocks[k])
            out.append(to_rows(seg, *blocks[k])[0])
        tail = [row[starts[k] : starts[k] + piece_len[k]] for k in GAIN_SEGMENTS]
        tail.append(jnp.zeros((128 - gain_width,), row.dtype))
        out.append(jnp.concatenate(tail).reshape(1, 128))
        out.append(jnp.zeros((rows - used_rows, 128), row.dtype))
        return jnp.concatenate(out, axis=0)

    def to_flat(block):
        out = []
        for k in range(11):
            r0, r1, l0, l1 = segments[k]
            if l0 is None:
                seg = from_rows(block[r0:r1].reshape(1, r1 - r0, 128), *blocks[k])
                out.append(seg.reshape(-1))
            else:
                out.append(block[r0, l0:l1])
        return jnp.concatenate(out).reshape(1, -1)

    grad = summed.reshape(rows, 128).astype(jnp.float32)
    weight_p = to_packed(weights.reshape(-1))
    first_p = to_packed(first_moment.reshape(-1))
    second_p = to_packed(second_moment.reshape(-1))
    new_first = 0.9 * first_p + 0.1 * grad
    new_second = 0.999 * second_p + 0.001 * grad * grad
    position = (
        lax.broadcasted_iota(jnp.int32, (rows, 128), 0) * 128
        + lax.broadcasted_iota(jnp.int32, (rows, 128), 1)
    )
    big_end = min(packed_start[k] for k in GAIN_SEGMENTS)
    update = new_first / (jnp.sqrt(new_second) + 1e-06)
    update = jnp.where(position < big_end, update + 0.01 * weight_p, update)
    new_weights, rounded = apply_step(weight_p, update, tuple(segments))
    _, first_p, second_p, grad = lax.optimization_barrier((rounded, first_p, second_p, grad))
    new_first = 0.9 * first_p + 0.1 * grad
    new_second = 0.999 * second_p + 0.001 * grad * grad
    gathered = lax.all_gather(rounded, "dp", axis=0, tiled=False)
    copies = [None] * 11
    for k in range(11):
        r0, r1, l0, l1 = segments[k]
        if l0 is None:
            part = from_rows(gathered[:, r0:r1, :], *blocks[k])
        else:
            part = gathered[:, r0, l0:l1]
        copies[k] = part.reshape(shapes[k])
    return (
        to_flat(new_weights),
        to_flat(new_first),
        to_flat(new_second),
        *copies,
    )


def solution(mesh):
    return jax.shard_map(
        on_device,
        mesh=mesh,
        in_specs=(
            P("dp", "tensor"),
            P("dp", None, "tensor"),
            P("dp", None, "tensor"),
            P("dp", None, "tensor"),
            P("dp", "tensor"),
            P("dp", None, "tensor"),
            P("dp", "tensor", None),
            P("dp", "tensor"),
            P("dp", None, "tensor"),
            P("dp", None, "tensor"),
            P("dp", "tensor", None),
            P("tensor", "dp"),
            P("tensor", "dp"),
            P("tensor", "dp"),
        ),
        out_specs=(
            P("tensor", "dp"),
            P("tensor", "dp"),
            P("tensor", "dp"),
            P("tensor"),
            P(None, "tensor"),
            P(None, "tensor"),
            P(None, "tensor"),
            P("tensor"),
            P(None, "tensor"),
            P("tensor", None),
            P("tensor"),
            P(None, "tensor"),
            P(None, "tensor"),
            P("tensor", None),
        ),
        check_vma=False,
    )
```

```python
import functools

import jax
import jax.numpy as jnp
from jax import lax
from jax.experimental import pallas as pl
from jax.experimental.pallas import tpu as pltpu
from jax.sharding import PartitionSpec as P

MESH = pl.DeviceIdType.MESH

GAIN_SEGMENTS = (0, 4, 7)


def apply_kernel(nd, nt, segments, weight_ref, update_ref, new_ref, low_ref, *scratch):
    recv_a, recv_b, send_a, got_a, send_b, got_b = scratch
    d = lax.axis_index("dp")
    t = lax.axis_index("tensor")
    barrier = pltpu.get_barrier_semaphore()
    for step in range(1, nt):
        pl.semaphore_signal(
            barrier, inc=1, device_id=(d, lax.rem(t + step, nt)), device_id_type=MESH
        )
    for step in range(1, nd):
        pl.semaphore_signal(
            barrier, inc=1, device_id=(lax.rem(d + step, nd), t), device_id_type=MESH
        )
    row = lax.broadcasted_iota(jnp.int32, (8, 128), 0)
    lane = lax.broadcasted_iota(jnp.int32, (8, 128), 1)

    def total(x):
        return jnp.sum(jnp.sum(x, axis=0, keepdims=True), axis=1, keepdims=True)

    def pick(vec, k):
        return total(jnp.where((row == 0) & (lane == k), vec, 0.0))

    vec = jnp.zeros((8, 128), jnp.float32)
    for k, (r0, r1, l0, l1) in enumerate(segments):
        if l0 is None:
            acc_w = jnp.zeros((8, 128), jnp.float32)
            acc_u = jnp.zeros((8, 128), jnp.float32)
            for r in range(r0, r1, 32):
                w = weight_ref[r : r + 32, :]
                u = update_ref[r : r + 32, :]
                acc_w = acc_w + jnp.sum((w * w).reshape(4, 8, 128), axis=0)
                acc_u = acc_u + jnp.sum((u * u).reshape(4, 8, 128), axis=0)
        else:
            keep = (row == 0) & (lane >= l0) & (lane < l1)
            w = weight_ref[r0 : r0 + 8, :]
            u = update_ref[r0 : r0 + 8, :]
            acc_w = jnp.where(keep, w * w, 0.0)
            acc_u = jnp.where(keep, u * u, 0.0)
        vec = jnp.where((row == 0) & (lane == k), total(acc_w), vec)
        vec = jnp.where((row == 1) & (lane == k), total(acc_u), vec)
    pl.semaphore_wait(barrier, nt - 1 + nd - 1)
    recv_a[t] = vec
    copies = []
    for step in range(1, nt):
        copy = pltpu.make_async_remote_copy(
            src_ref=recv_a.at[t],
            dst_ref=recv_a.at[t],
            send_sem=send_a.at[step],
            recv_sem=got_a.at[t],
            device_id=(d, lax.rem(t + step, nt)),
            device_id_type=MESH,
        )
        copy.start()
        copies.append(copy)
    for step in range(1, nt):
        source = lax.rem(t + nt - step, nt)
        pltpu.make_async_remote_copy(
            src_ref=recv_a.at[source],
            dst_ref=recv_a.at[source],
            send_sem=send_a.at[step],
            recv_sem=got_a.at[source],
            device_id=(d, source),
            device_id_type=MESH,
        ).wait_recv()
    for copy in copies:
        copy.wait_send()
    acc = recv_a[0]
    for slot in range(1, nt):
        acc = acc + recv_a[slot]
    recv_b[d] = acc
    copies = []
    for step in range(1, nd):
        copy = pltpu.make_async_remote_copy(
            src_ref=recv_b.at[d],
            dst_ref=recv_b.at[d],
            send_sem=send_b.at[step],
            recv_sem=got_b.at[d],
            device_id=(lax.rem(d + step, nd), t),
            device_id_type=MESH,
        )
        copy.start()
        copies.append(copy)
    for step in range(1, nd):
        source = lax.rem(d + nd - step, nd)
        pltpu.make_async_remote_copy(
            src_ref=recv_b.at[source],
            dst_ref=recv_b.at[source],
            send_sem=send_b.at[step],
            recv_sem=got_b.at[source],
            device_id=(source, t),
            device_id_type=MESH,
        ).wait_recv()
    for copy in copies:
        copy.wait_send()
    acc = recv_b[0]
    for slot in range(1, nd):
        acc = acc + recv_b[slot]
    trust = jnp.sqrt(acc[0:1, :]) / jnp.sqrt(acc[1:2, :])
    trust = jnp.broadcast_to(trust, (8, 128))
    gain_scale = jnp.zeros((8, 128), jnp.float32)
    for k, (r0, r1, l0, l1) in enumerate(segments):
        factor = 0.1 * pick(trust, k)
        if l0 is None:
            for r in range(r0, r1, 32):
                w = weight_ref[r : r + 32, :]
                u = update_ref[r : r + 32, :]
                new = w - factor * u
                new_ref[r : r + 32, :] = new
                low_ref[r : r + 32, :] = new.astype(low_ref.dtype)
        else:
            gain_scale = jnp.where((lane >= l0) & (lane < l1), factor, gain_scale)
            tail = r0
    for r in range(tail, weight_ref.shape[0], 8):
        w = weight_ref[r : r + 8, :]
        u = update_ref[r : r + 8, :]
        scale = gain_scale if r == tail else jnp.zeros((8, 128), jnp.float32)
        new = w - scale * u
        new_ref[r : r + 8, :] = new
        low_ref[r : r + 8, :] = new.astype(low_ref.dtype)


def pack_kernel(plan, *refs):
    out_ref = refs[-1]
    for index, (r0, a, b, raw) in enumerate(plan):
        src = refs[index]
        if raw:
            for rt in range(a // 8):
                for ct in range(b // 128):
                    at = r0 + (rt * (b // 128) + ct) * 8
                    out_ref[0, at : at + 8, :] = src[
                        0, rt * 8 : (rt + 1) * 8, ct * 128 : (ct + 1) * 128
                    ]
        else:
            out_ref[0, r0 : r0 + a, :] = src[0]


def pack_rows(inputs, plan, owners, rows):
    specs = []
    for x, (r0, a, b, raw) in zip(inputs, plan):
        if raw:
            specs.append(pl.BlockSpec((1, a, b), lambda j: (0, j, 0)))
        else:
            specs.append(pl.BlockSpec((1, a, 128), lambda j: (j, 0, 0)))
    return pl.pallas_call(
        functools.partial(pack_kernel, plan),
        grid=(owners,),
        out_shape=jax.ShapeDtypeStruct((owners, rows, 128), jnp.bfloat16),
        in_specs=specs,
        out_specs=pl.BlockSpec((1, rows, 128), lambda j: (j, 0, 0)),
    )(*inputs)


def apply_step(weight_p, update, segments):
    nd = lax.axis_size("dp")
    nt = lax.axis_size("tensor")
    return pl.pallas_call(
        functools.partial(apply_kernel, nd, nt, segments),
        out_shape=(
            jax.ShapeDtypeStruct(weight_p.shape, jnp.float32),
            jax.ShapeDtypeStruct(weight_p.shape, jnp.bfloat16),
        ),
        in_specs=[pl.BlockSpec(memory_space=pltpu.VMEM)] * 2,
        out_specs=(
            pl.BlockSpec(memory_space=pltpu.VMEM),
            pl.BlockSpec(memory_space=pltpu.VMEM),
        ),
        scratch_shapes=[
            pltpu.VMEM((nt, 8, 128), jnp.float32),
            pltpu.VMEM((nd, 8, 128), jnp.float32),
            pltpu.SemaphoreType.DMA((nt,)),
            pltpu.SemaphoreType.DMA((nt,)),
            pltpu.SemaphoreType.DMA((nd,)),
            pltpu.SemaphoreType.DMA((nd,)),
        ],
        compiler_params=pltpu.CompilerParams(collective_id=0, has_side_effects=True),
    )(weight_p, update)


def on_device(*args):
    grads = args[:11]
    weights, first_moment, second_moment = args[11:]
    owners = lax.axis_size("dp")
    shapes = [g.shape[1:] for g in grads]
    pieces = [g.reshape(owners, -1) for g in grads]
    piece_len = [p.shape[1] for p in pieces]
    starts = [sum(piece_len[:k]) for k in range(11)]
    order = [k for k in range(11) if k not in GAIN_SEGMENTS] + list(GAIN_SEGMENTS)
    packed_len = sum(piece_len)
    padded = -(-packed_len // 1024) * 1024
    rows = padded // 128
    blocks = [(g.shape[1] // owners, g.shape[2]) if g.ndim == 3 else None for g in grads]

    def to_rows(x, a, b):
        lead = x.shape[0]
        if a % 8 == 0 and b % 128 == 0:
            x = x.reshape(lead, a // 8, 8, b // 128, 128).transpose(0, 1, 3, 2, 4)
            return x.reshape(lead, a * b // 128, 128)
        if b % 128 != 0 and a == 128:
            return x.transpose(0, 2, 1)
        return x.reshape(lead, a * b // 128, 128)

    def from_rows(y, a, b):
        lead = y.shape[0]
        if a % 8 == 0 and b % 128 == 0:
            y = y.reshape(lead, a // 8, b // 128, 8, 128).transpose(0, 1, 3, 2, 4)
            return y.reshape(lead, a, b)
        if b % 128 != 0 and a == 128:
            return y.transpose(0, 2, 1)
        return y.reshape(lead, a, b)

    big = [k for k in order if k not in GAIN_SEGMENTS]
    inputs = []
    plan = []
    row = 0
    for k in big:
        a, b = blocks[k]
        if a % 16 == 0 and b % 128 == 0:
            inputs.append(grads[k])
            plan.append((row, a, b, True))
        else:
            inputs.append(to_rows(grads[k][0].reshape((owners,) + blocks[k]), a, b))
            plan.append((row, a * b // 128, 128, False))
        row += a * b // 128
    gains = jnp.concatenate([pieces[k] for k in GAIN_SEGMENTS], axis=1)
    gain_width = gains.shape[1]
    used_rows = row + 1
    tail = jnp.pad(gains, ((0, 0), (0, 128 - gain_width))).reshape(owners, 1, 128)
    tail = jnp.pad(tail, ((0, 0), (0, rows - used_rows), (0, 0)))
    inputs.append(tail)
    plan.append((row, rows - row, 128, False))
    flat = pack_rows(inputs, tuple(plan), owners, rows)
    summed = lax.psum_scatter(flat, "dp", scatter_dimension=0, tiled=True)
    summed = lax.optimization_barrier(summed).reshape(-1)
    packed_start = {}
    offset = 0
    for k in order:
        packed_start[k] = offset
        offset += piece_len[k]
    segments = []
    for k in range(11):
        a, b = packed_start[k], packed_start[k] + piece_len[k]
        if a % 128 == 0 and b % 128 == 0:
            segments.append((a // 128, b // 128, None, None))
        else:
            segments.append((a // 128, a // 128 + 1, a % 128, (b - 1) % 128 + 1))

    def to_packed(row):
        out = []
        for k in big:
            seg = row[starts[k] : starts[k] + piece_len[k]].reshape((1,) + blocks[k])
            out.append(to_rows(seg, *blocks[k])[0])
        tail = [row[starts[k] : starts[k] + piece_len[k]] for k in GAIN_SEGMENTS]
        tail.append(jnp.zeros((128 - gain_width,), row.dtype))
        out.append(jnp.concatenate(tail).reshape(1, 128))
        out.append(jnp.zeros((rows - used_rows, 128), row.dtype))
        return jnp.concatenate(out, axis=0)

    def to_flat(block):
        out = []
        for k in range(11):
            r0, r1, l0, l1 = segments[k]
            if l0 is None:
                seg = from_rows(block[r0:r1].reshape(1, r1 - r0, 128), *blocks[k])
                out.append(seg.reshape(-1))
            else:
                out.append(block[r0, l0:l1])
        return jnp.concatenate(out).reshape(1, -1)

    grad = summed.reshape(rows, 128).astype(jnp.float32)
    weight_p = to_packed(weights.reshape(-1))
    first_p = to_packed(first_moment.reshape(-1))
    second_p = to_packed(second_moment.reshape(-1))
    new_first = 0.9 * first_p + 0.1 * grad
    new_second = 0.999 * second_p + 0.001 * grad * grad
    position = (
        lax.broadcasted_iota(jnp.int32, (rows, 128), 0) * 128
        + lax.broadcasted_iota(jnp.int32, (rows, 128), 1)
    )
    big_end = min(packed_start[k] for k in GAIN_SEGMENTS)
    update = new_first / (jnp.sqrt(new_second) + 1e-06)
    update = jnp.where(position < big_end, update + 0.01 * weight_p, update)
    new_weights, rounded = apply_step(weight_p, update, tuple(segments))
    _, first_p, second_p, grad = lax.optimization_barrier((rounded, first_p, second_p, grad))
    new_first = 0.9 * first_p + 0.1 * grad
    new_second = 0.999 * second_p + 0.001 * grad * grad
    gathered = lax.all_gather(rounded, "dp", axis=0, tiled=False)
    copies = [None] * 11
    for k in range(11):
        r0, r1, l0, l1 = segments[k]
        if l0 is None:
            part = from_rows(gathered[:, r0:r1, :], *blocks[k])
        else:
            part = gathered[:, r0, l0:l1]
        copies[k] = part.reshape(shapes[k])
    return (
        to_flat(new_weights),
        to_flat(new_first),
        to_flat(new_second),
        *copies,
    )


def solution(mesh):
    return jax.shard_map(
        on_device,
        mesh=mesh,
        in_specs=(
            P("dp", "tensor"),
            P("dp", None, "tensor"),
            P("dp", None, "tensor"),
            P("dp", None, "tensor"),
            P("dp", "tensor"),
            P("dp", None, "tensor"),
            P("dp", "tensor", None),
            P("dp", "tensor"),
            P("dp", None, "tensor"),
            P("dp", None, "tensor"),
            P("dp", "tensor", None),
            P("tensor", "dp"),
            P("tensor", "dp"),
            P("tensor", "dp"),
        ),
        out_specs=(
            P("tensor", "dp"),
            P("tensor", "dp"),
            P("tensor", "dp"),
            P("tensor"),
            P(None, "tensor"),
            P(None, "tensor"),
            P(None, "tensor"),
            P("tensor"),
            P(None, "tensor"),
            P("tensor", None),
            P("tensor"),
            P(None, "tensor"),
            P(None, "tensor"),
            P("tensor", None),
        ),
        check_vma=False,
    )
```
